32 devices in a mesh: ta: 4 (over z), ha: 4 (over y, x), wa: 2 (over core).
Axes of the slice: x: 2, y: 2, z: 4, core: 2. Of those that a mesh axis runs over, the one named last changes fastest.
Arguments:
- queries: bfloat16 [16, 16, 4, 4, 1536], P('ta', 'ha', 'wa'), may hold values from -4.5 to 4.5
- key_states: bfloat16 [16, 16, 4, 4, 1536], P('ta', 'ha', 'wa'), may hold values from -4.5 to 4.5
- value_states: bfloat16 [16, 16, 4, 4, 1536], P('ta', 'ha', 'wa'), may hold values from -6 to 6
- output_cotangent: bfloat16 [16, 16, 4, 4, 1536], P('ta', 'ha', 'wa'), may hold values from -48 to 48
- tile_valid: int32 [16, 16, 4], replicated, may hold values from 0 to 1, as said below
- window_radius: int32 [12, 3], replicated, may hold values from 0 to 1
Outputs:
- query_gradient: bfloat16 [16, 16, 4, 4, 1536], P('ta', 'ha', 'wa')
- key_gradient: bfloat16 [16, 16, 4, 4, 1536], P('ta', 'ha', 'wa')
- value_gradient: bfloat16 [16, 16, 4, 4, 1536], P('ta', 'ha', 'wa')
The draws below stay inside these ranges and needn't reach their ends.
Inputs may be any that keep to these rules, and one draw needn't show every extreme that they name: `tile_valid`: 0 exactly on the first zero or one and the last zero to two tile layers along each axis (padding at the clip's borders), with at least one such layer in all, 1 everywhere else.
All inputs are finite; a program needn't handle non-finite values.
Results may differ from the reference program's by a relative error of at most 0.0084.
Values may be sent and summed in bfloat16 or wider, within the bound.
No kernel may reach another device: no remote copies, remote signals or barrier semaphores. Data moves between devices by JAX's collectives and lax.ppermute only.
A program may use at most 64 MiB of HBM per device.

```python
import math
import jax
import jax.numpy as jnp
from jax import lax

HEADS = 12
HD = 128
WIDTH = 1536
TILE = 4
BT = 4
BH = 4
BW = 2
GT = 16
GH = 16
GW = 4
N_TA = 4
N_HA = 4
N_WA = 2


def draw_queries(key, part):
    full_shape = (GT, GH, GW, TILE, WIDTH)
    result = jnp.clip(jax.random.normal(jax.random.fold_in(key, 11), full_shape, jnp.float32), -4.5, 4.5)
    return result.astype(jnp.bfloat16)


def draw_key_states(key, part):
    full_shape = (GT, GH, GW, TILE, WIDTH)
    result = jnp.clip(jax.random.normal(jax.random.fold_in(key, 12), full_shape, jnp.float32), -4.5, 4.5)
    return result.astype(jnp.bfloat16)


def draw_tile_valid(key, part):
    leading = jax.random.randint(jax.random.fold_in(key, 8101), (3,), 0, 2).astype(jnp.int32)
    trailing = jax.random.randint(jax.random.fold_in(key, 8102), (3,), 0, 3).astype(jnp.int32)
    none_set = 1 - jnp.minimum(jnp.sum(leading) + jnp.sum(trailing), 1)
    trailing = trailing.at[2].set(jnp.maximum(trailing[2], none_set))
    time_index = jnp.arange(GT, dtype=jnp.int32)
    row_index = jnp.arange(GH, dtype=jnp.int32)
    column_index = jnp.arange(GW, dtype=jnp.int32)
    time_pad = ((time_index < leading[0]) | (time_index >= GT - trailing[0])).astype(jnp.int32)
    row_pad = ((row_index < leading[1]) | (row_index >= GH - trailing[1])).astype(jnp.int32)
    column_pad = ((column_index < leading[2]) | (column_index >= GW - trailing[2])).astype(jnp.int32)
    padding = jnp.maximum(jnp.maximum(time_pad[:, None, None], row_pad[None, :, None]), column_pad[None, None, :])
    return (1 - padding).astype(jnp.int32)


def touch_ends(drawn, own_key, least, largest):
    place = [jax.random.randint(jax.random.fold_in(own_key, axis), (), 0, length) for axis, length in enumerate(drawn.shape)]
    widest = drawn.shape.index(max(drawn.shape))
    neighbour = place[:widest] + [(place[widest] + 1) % drawn.shape[widest]] + place[widest + 1:]
    return drawn.at[tuple(place)].set(least).at[tuple(neighbour)].set(largest)


def level_of(rng, shape, shards, low, top_value):
    factor_of = 1.0
    for position, shards_of in shards:
        heights = jax.random.uniform(jax.random.fold_in(jax.random.fold_in(rng, 6), position), (shards_of,), jnp.float32, low / len(shards), top_value / len(shards))
        factor_of = factor_of * jnp.repeat(jnp.exp(heights), shape[position] // shards_of).reshape((-1,) + (1,) * (len(shape) - 1 - position))
    return factor_of


def gaussian(stream_key, shape, deviation, bound, cuts=(), kind=jnp.bfloat16):
    values = deviation * jax.random.normal(stream_key, shape, jnp.float32)
    if cuts:
        values = values * level_of(stream_key, shape, cuts, -0.22, 0.18)
    return jnp.clip(values, -bound, bound).astype(kind)


def setup_inputs(seed: int = 0) -> dict:
    seeds = jax.random.split(jax.random.key(seed), 7)
    return {
        "queries": draw_queries(jax.random.fold_in(seeds[6], 71), 0),
        "key_states": draw_key_states(jax.random.fold_in(seeds[6], 71), 0),
        "value_states": gaussian(seeds[2], (GT, GH, GW, TILE, WIDTH), 1.0, 6.0, ((0, 4), (1, 4), (2, 2))),
        "output_cotangent": gaussian(seeds[3], (GT, GH, GW, TILE, WIDTH), 8.0, 48.0, ((0, 4), (1, 4), (2, 2))),
        "tile_valid": draw_tile_valid(jax.random.fold_in(seeds[6], 71), 0),
        "window_radius": touch_ends(jax.random.randint(seeds[5], (HEADS, 3), 0, 2), jax.random.fold_in(seeds[5], 1), 0, 1).astype(jnp.int32),
    }


NEG_FILL = -1e+30

def axis_window(query_coords, key_coords, radius, grid_length):
    window_start = query_coords[None, :] - radius[:, None]
    window_span = 2 * radius + 1
    above_start = key_coords[None, None, :] >= window_start[:, :, None]
    below_end = key_coords[None, None, :] < window_start[:, :, None] + window_span[:, None, None]
    inside = (query_coords >= 0) & (query_coords < grid_length)
    key_inside = (key_coords >= 0) & (key_coords < grid_length)
    return above_start & below_end & inside[None, :, None] & key_inside[None, None, :]

def tile_mask(query_coords, key_coords, window_radius, grid_sizes, key_valid):
    time_window = axis_window(query_coords[0], key_coords[0], window_radius[:, 0], grid_sizes[0])
    row_window = axis_window(query_coords[1], key_coords[1], window_radius[:, 1], grid_sizes[1])
    column_window = axis_window(query_coords[2], key_coords[2], window_radius[:, 2], grid_sizes[2])
    within = time_window[:, :, None, None, :, None, None] & row_window[:, None, :, None, None, :, None] & column_window[:, None, None, :, None, None, :]
    time_same = query_coords[0][:, None] == key_coords[0][None, :]
    row_same = query_coords[1][:, None] == key_coords[1][None, :]
    column_same = query_coords[2][:, None] == key_coords[2][None, :]
    same_tile = time_same[:, None, None, :, None, None] & row_same[None, :, None, None, :, None] & column_same[None, None, :, None, None, :]
    usable = key_valid[None, None, None, :, :, :] | same_tile
    allowed = within & usable[None]
    head_count = window_radius.shape[0]
    query_tiles = query_coords[0].shape[0] * query_coords[1].shape[0] * query_coords[2].shape[0]
    key_tiles = key_coords[0].shape[0] * key_coords[1].shape[0] * key_coords[2].shape[0]
    return allowed.reshape(head_count, query_tiles, key_tiles)

def expand_mask(scores, allowed, tile_cells):
    group_count, row_count, column_count = scores.shape
    shaped = scores.reshape(group_count, row_count // tile_cells, tile_cells, column_count // tile_cells, tile_cells)
    shaped = jnp.where(allowed[:, :, None, :, None], shaped, NEG_FILL)
    return shaped.reshape(group_count, row_count, column_count)

def round_low(values):
    return lax.optimization_barrier(values.astype(jnp.bfloat16)).astype(jnp.float32)

def reference(queries, key_states, value_states, output_cotangent, tile_valid, window_radius):
    score_scale = 1.0 / math.sqrt(HD)
    grid_sizes = (GT, GH, GW)
    block_count = N_TA * N_HA * N_WA
    own_count = BT * BH * BW * TILE
    zero_index = jnp.zeros((), jnp.int32)
    pad_widths = ((1, 1), (1, 1), (1, 1), (0, 0), (0, 0))
    padded_queries = jnp.pad(queries, pad_widths)
    padded_keys = jnp.pad(key_states, pad_widths)
    padded_values = jnp.pad(value_states, pad_widths)
    padded_cotangent = jnp.pad(output_cotangent, pad_widths)
    valid_padded = jnp.pad(tile_valid, 1)

    def corners(index):
        time_block = index // (N_HA * N_WA)
        row_block = index // N_WA % N_HA
        column_block = index % N_WA
        return ((time_block * BT).astype(jnp.int32), (row_block * BH).astype(jnp.int32), (column_block * BW).astype(jnp.int32))

    def block_coords(anchors, margin):
        return (anchors[0] - margin + jnp.arange(BT + 2 * margin, dtype=jnp.int32), anchors[1] - margin + jnp.arange(BH + 2 * margin, dtype=jnp.int32), anchors[2] - margin + jnp.arange(BW + 2 * margin, dtype=jnp.int32))

    def cut_block(array, anchors, margin):
        lengths = (BT + 2 * margin, BH + 2 * margin, BW + 2 * margin) + tuple(array.shape[3:])
        starts = tuple(anchors) + (zero_index,) * (array.ndim - 3)
        return lax.dynamic_slice(array, starts, lengths)

    def first_pass(index):
        anchors = corners(index)
        own_queries = cut_block(queries, anchors, 0).astype(jnp.float32).reshape(own_count, HEADS, HD)
        own_cotangent = cut_block(output_cotangent, anchors, 0).astype(jnp.float32).reshape(own_count, HEADS, HD)
        outer_keys = cut_block(padded_keys, anchors, 1).astype(jnp.float32).reshape(-1, HEADS, HD)
        outer_values = cut_block(padded_values, anchors, 1).astype(jnp.float32).reshape(-1, HEADS, HD)
        outer_valid = cut_block(valid_padded, anchors, 1) > 0
        allowed = tile_mask(block_coords(anchors, 0), block_coords(anchors, 1), window_radius, grid_sizes, outer_valid)
        scores = jnp.einsum('qhd,khd->hqk', own_queries, outer_keys) * score_scale
        scores = expand_mask(scores, allowed, TILE)
        row_peak = lax.optimization_barrier(jnp.max(scores, axis=2, keepdims=True))
        logsum = row_peak + jnp.log(lax.optimization_barrier(jnp.sum(jnp.exp(scores - row_peak), axis=2, keepdims=True)))
        attention = jnp.exp(scores - logsum)
        weights_low = round_low(attention)
        output = jnp.einsum('hqk,khd->qhd', weights_low, outer_values)
        drift = lax.optimization_barrier(jnp.sum(own_cotangent * output, axis=2))
        weight_grads = jnp.einsum('qhd,khd->hqk', own_cotangent, outer_values)
        score_grads = round_low(attention * (weight_grads - drift.T[:, :, None]))
        query_gradient = jnp.einsum('hqk,khd->qhd', score_grads, outer_keys) * score_scale
        return (query_gradient.astype(jnp.bfloat16).reshape(BT, BH, BW, TILE, WIDTH), logsum[:, :, 0].T.reshape(BT, BH, BW, TILE, HEADS), drift.reshape(BT, BH, BW, TILE, HEADS))

    def assemble(stacked):
        rest = tuple(stacked.shape[4:])
        shaped = stacked.reshape((N_TA, N_HA, N_WA, BT, BH, BW) + rest)
        shaped = jnp.transpose(shaped, (0, 3, 1, 4, 2, 5) + tuple(range(6, 6 + len(rest))))
        return shaped.reshape((GT, GH, GW) + rest)
    block_ids = jnp.arange(block_count, dtype=jnp.int32)
    query_blocks, logsum_blocks, drift_blocks = lax.map(first_pass, block_ids)
    query_gradient = assemble(query_blocks)
    padded_logsum = jnp.pad(assemble(logsum_blocks), pad_widths)
    padded_drift = jnp.pad(assemble(drift_blocks), pad_widths)

    def second_pass(index):
        anchors = corners(index)
        own_keys = cut_block(key_states, anchors, 0).astype(jnp.float32).reshape(own_count, HEADS, HD)
        own_values = cut_block(value_states, anchors, 0).astype(jnp.float32).reshape(own_count, HEADS, HD)
        outer_queries = cut_block(padded_queries, anchors, 1).astype(jnp.float32).reshape(-1, HEADS, HD)
        outer_cotangent = cut_block(padded_cotangent, anchors, 1).astype(jnp.float32).reshape(-1, HEADS, HD)
        outer_logsum = cut_block(padded_logsum, anchors, 1).reshape(-1, HEADS)
        outer_drift = cut_block(padded_drift, anchors, 1).reshape(-1, HEADS)
        own_valid = cut_block(tile_valid, anchors, 0) > 0
        allowed = tile_mask(block_coords(anchors, 1), block_coords(anchors, 0), window_radius, grid_sizes, own_valid)
        scores = jnp.einsum('qhd,khd->hqk', outer_queries, own_keys) * score_scale
        scores = expand_mask(scores, allowed, TILE)
        attention = jnp.exp(scores - outer_logsum.T[:, :, None])
        weights_low = round_low(attention)
        weight_grads = jnp.einsum('qhd,khd->hqk', outer_cotangent, own_values)
        score_grads = round_low(attention * (weight_grads - outer_drift.T[:, :, None]))
        key_gradient = jnp.einsum('hqk,qhd->khd', score_grads, outer_queries) * score_scale
        value_gradient = jnp.einsum('hqk,qhd->khd', weights_low, outer_cotangent)
        return (key_gradient.astype(jnp.bfloat16).reshape(BT, BH, BW, TILE, WIDTH), value_gradient.astype(jnp.bfloat16).reshape(BT, BH, BW, TILE, WIDTH))
    key_blocks, value_blocks = lax.map(second_pass, block_ids)
    return (query_gradient, assemble(key_blocks), assemble(value_blocks))
```

```python
import functools
import math

import jax
import jax.numpy as jnp
import numpy as np
from jax import lax
from jax.experimental import pallas as pl
from jax.experimental.pallas import tpu as pltpu
from jax.sharding import PartitionSpec as P

NEG = -1e30
LOG2E = 1.4426950408889634
EVEN, ODD = 1000, 1001
AXES = ("ta", "ha", "wa")


def matchings(n):
    even = [(i, i ^ 1) for i in range(n) if (i ^ 1) < n]
    odd = [(i, ((i + 1) ^ 1) - 1) for i in range(n) if 0 <= ((i + 1) ^ 1) - 1 < n]
    return [m for m in (even, odd) if m]


def exchange(axis, first, last):
    n = lax.axis_size(axis)
    is_odd = lax.rem(lax.axis_index(axis), 2) == 1
    pieces = []
    for k, pairs in enumerate(matchings(n)):
        flip = is_odd if k == 0 else jnp.logical_not(is_odd)
        pieces.append(lax.ppermute(jnp.where(flip, first, last), axis, pairs))
    return pieces


def halo(own, block):
    T, H, W, C = block
    k, _, width = own.shape
    grid = own.reshape(k, W, T, H, C, width)
    ha = exchange(
        "ha",
        grid[:, :, :, 0].reshape(k, W * T * C, width),
        grid[:, :, :, H - 1].reshape(k, W * T * C, width),
    )
    own_t = own.reshape(k, W, T, H * C, width)
    ha_t = [p.reshape(k, W, T, C, width) for p in ha]

    def time_layer(t):
        return jnp.concatenate([own_t[:, :, t]] + [p[:, :, t] for p in ha_t], axis=2).reshape(
            k, -1, width
        )

    ta = exchange("ta", time_layer(0), time_layer(T - 1))

    def column(w):
        return jnp.concatenate(
            [p.reshape(k, W, -1, width)[:, w] for p in [own] + ha + ta], axis=1
        )

    wa = exchange("wa", column(0), column(W - 1))
    return ha + ta + wa


def piece_coords(block, counts):
    T, H, W, C = block
    marks = (EVEN, ODD)

    def rows(cells):
        return [np.repeat(np.array(cells, np.int32), C, axis=0)]

    own = [[[(t, h, w) for h in range(H)] for t in range(T)] for w in range(W)]
    pieces = [np.array(own, np.int32).reshape(W, -1, 3)]
    for m in marks[: counts[1]]:
        pieces.append(np.array([[(t, m, w) for t in range(T)] for w in range(W)], np.int32))
    hs = list(range(H)) + list(marks[: counts[1]])
    for m in marks[: counts[0]]:
        pieces.append(np.array([[(m, h, w) for h in hs] for w in range(W)], np.int32))
    column = np.concatenate([p[0] for p in pieces], axis=0)
    out = [p.reshape(-1, 3) for p in pieces]
    for m in marks[: counts[2]]:
        c = column.copy()
        c[:, 2] = m
        out.append(c)
    return np.repeat(np.concatenate(out, axis=0), C, axis=0)


def build_code(oc_ref, kc_ref, bounds_ref, code_ref, block, grids, own_is_query):
    bad = None
    same = None
    valid = None
    code = None
    for a, axis in enumerate(AXES):
        index = lax.axis_index(axis)
        length = block[a]
        odd = lax.rem(index, 2)
        at_even = jnp.where(odd == 1, -1, length)
        at_odd = jnp.where(odd == 1, length, -1)
        own = oc_ref[:, a : a + 1]
        outer = kc_ref[a : a + 1, :]
        outer = jnp.where(outer == EVEN, at_even, jnp.where(outer == ODD, at_odd, outer))
        place = outer + index * length
        inside = (place >= 0) & (place < grids[a])
        low, high = bounds_ref[2 * a], bounds_ref[2 * a + 1]
        checked = own + index * length if not own_is_query else place
        ok = (checked >= low) & (checked <= high)
        apart = jnp.abs(own - outer)
        here_bad = jnp.where((apart > 1) | jnp.logical_not(inside), 8, 0)
        here_code = jnp.where(apart == 1, 1 << a, 0)
        code = here_code if code is None else code | here_code
        bad = here_bad if bad is None else bad | here_bad
        valid = jnp.where(ok, 0, 8) if valid is None else valid | jnp.where(ok, 0, 8)
        same = apart if same is None else same | apart
    blocked = jnp.where(same == 0, 0, jnp.broadcast_to(valid, same.shape))
    code_ref[...] = code | bad | blocked


def forbidden(radius_ref, h):
    bits = 8
    for a in range(3):
        bits = bits + (1 - radius_ref[h, a]) * (1 << a)
    return bits


NT = (((1,), (1,)), ((), ()))
NN = (((1,), (0,)), ((), ()))


def dot(a, b, dims):
    return lax.dot_general(a, b, dims, preferred_element_type=jnp.float32)


def gather(refs, which, cols, pad):
    parts = [r[which, :, cols] for r in refs]
    if pad:
        parts.append(jnp.zeros((pad, parts[0].shape[1]), parts[0].dtype))
    return jnp.concatenate(parts, axis=0)


def query_kernel(cfg, radius_ref, bounds_ref, oc_ref, kc_ref, qd_ref, *rest):
    block, grids, heads, depth, pad, count = cfg
    kv = rest[:count]
    dq_ref, stat_ref, code_ref = rest[count:]
    build_code(oc_ref, kc_ref, bounds_ref, code_ref, block, grids, True)
    scale = 1.0 / math.sqrt(depth)
    rows = qd_ref.shape[1]
    lane = lax.broadcasted_iota(jnp.int32, (rows, stat_ref.shape[1]), 1)
    stats = jnp.zeros((rows, stat_ref.shape[1]), jnp.float32)
    for h in range(heads):
        cols = slice(h * depth, (h + 1) * depth)
        keys = gather(kv, 0, cols, pad)
        values = gather(kv, 1, cols, pad)
        allowed = (code_ref[...] & forbidden(radius_ref, h)) == 0
        scores = dot(qd_ref[0, :, cols], keys, NT) * (scale * LOG2E)
        scores = jnp.where(allowed, scores, NEG)
        peak = jnp.max(scores, axis=1, keepdims=True)
        raised = jnp.exp2(scores - peak)
        logsum = peak + jnp.log2(jnp.sum(raised, axis=1, keepdims=True))
        attention = jnp.exp2(scores - logsum)
        grads = dot(qd_ref[1, :, cols], values, NT)
        low = attention.astype(jnp.bfloat16).astype(jnp.float32)
        drift = jnp.sum(low * grads, axis=1, keepdims=True)
        score_grads = (attention * (grads - drift)).astype(jnp.bfloat16)
        dq_ref[:, cols] = (dot(score_grads, keys, NN) * scale).astype(jnp.bfloat16)
        stats = jnp.where(lane == h, logsum, stats)
        stats = jnp.where(lane == heads + h, drift, stats)
    stat_ref[...] = stats


def key_kernel(cfg, radius_ref, bounds_ref, oc_ref, kc_ref, kv_ref, *rest):
    block, grids, heads, depth, pad, count = cfg
    qd = rest[:count]
    st = rest[count : 2 * count]
    dk_ref, dv_ref, code_ref, row_ref = rest[2 * count :]
    build_code(oc_ref, kc_ref, bounds_ref, code_ref, block, grids, False)
    scale = 1.0 / math.sqrt(depth)
    parts = [r[0] for r in st]
    if pad:
        parts.append(jnp.zeros((pad, parts[0].shape[1]), jnp.float32))
    row_ref[...] = jnp.concatenate(parts, axis=0).T
    for h in range(heads):
        cols = slice(h * depth, (h + 1) * depth)
        queries = gather(qd, 0, cols, pad)
        cotangent = gather(qd, 1, cols, pad)
        allowed = (code_ref[...] & forbidden(radius_ref, h)) == 0
        scores = dot(kv_ref[0, :, cols], queries, NT) * (scale * LOG2E)
        scores = jnp.where(allowed, scores, NEG)
        attention = jnp.exp2(scores - row_ref[h : h + 1, :])
        grads = dot(kv_ref[1, :, cols], cotangent, NT)
        score_grads = (attention * (grads - row_ref[heads + h : heads + h + 1, :])).astype(
            jnp.bfloat16
        )
        dk_ref[:, cols] = (dot(score_grads, queries, NN) * scale).astype(jnp.bfloat16)
        dv_ref[:, cols] = dot(attention.astype(jnp.bfloat16), cotangent, NN).astype(jnp.bfloat16)


def per_device(queries, key_states, value_states, output_cotangent, tile_valid, window_radius):
    T, H, W, C, width = queries.shape
    block = (T, H, W, C)
    heads = window_radius.shape[0]
    depth = width // heads
    sizes = tuple(lax.axis_size(a) for a in AXES)
    grids = tuple(n * b for n, b in zip(sizes, block))
    counts = tuple(len(matchings(n)) for n in sizes)
    rows = T * H * W * C

    def rowwise(x):
        return x.transpose(2, 0, 1, 3, 4).reshape(rows, width)

    def tilewise(x):
        return x.reshape(W, T, H, C, width).transpose(1, 2, 0, 3, 4)

    kv = jnp.stack([rowwise(key_states), rowwise(value_states)])
    qd = jnp.stack([rowwise(queries), rowwise(output_cotangent)])
    kv_pieces = [kv] + halo(kv, block)
    qd_pieces = [qd] + halo(qd, block)

    lines = (tile_valid[:, 1, 1], tile_valid[1, :, 1], tile_valid[1, 1, :])
    bounds = jnp.stack(
        [b for v in lines for b in (1 - v[0], v.shape[0] - 3 + v[-1] + v[-2])]
    ).astype(jnp.int32)

    coords = piece_coords(block, counts)
    total = coords.shape[0]
    padded = -(-total // 128) * 128
    pad = padded - total
    outer = np.full((8, padded), -(1 << 20), np.int32)
    outer[:3, :total] = coords.T
    inner = np.zeros((rows, 8), np.int32)
    inner[:, :3] = coords[:rows]
    cfg = (block, grids, heads, depth, pad, len(kv_pieces))
    smem = pl.BlockSpec(memory_space=pltpu.SMEM)
    vmem = pl.BlockSpec(memory_space=pltpu.VMEM)
    lanes = -(-2 * heads // 128) * 128
    params = pltpu.CompilerParams(vmem_limit_bytes=48 << 20)

    query_gradient, stats = pl.pallas_call(
        functools.partial(query_kernel, cfg),
        out_shape=(
            jax.ShapeDtypeStruct((rows, width), jnp.bfloat16),
            jax.ShapeDtypeStruct((rows, lanes), jnp.float32),
        ),
        in_specs=[smem] * 2 + [vmem] * (3 + len(kv_pieces)),
        out_specs=(vmem, vmem),
        scratch_shapes=[pltpu.VMEM((rows, padded), jnp.int32)],
        compiler_params=params,
        name="query_side",
    )(window_radius, bounds, inner, outer, qd, *kv_pieces)

    stats = stats[None]
    stat_pieces = [stats] + halo(stats, block)

    key_gradient, value_gradient = pl.pallas_call(
        functools.partial(key_kernel, cfg),
        out_shape=(jax.ShapeDtypeStruct((rows, width), jnp.bfloat16),) * 2,
        in_specs=[smem] * 2 + [vmem] * (3 + 2 * len(kv_pieces)),
        out_specs=(vmem, vmem),
        scratch_shapes=[
            pltpu.VMEM((rows, padded), jnp.int32),
            pltpu.VMEM((lanes, padded), jnp.float32),
        ],
        compiler_params=params,
        name="key_side",
    )(window_radius, bounds, inner, outer, kv, *qd_pieces, *stat_pieces)

    return (tilewise(query_gradient), tilewise(key_gradient), tilewise(value_gradient))


def solution(mesh):
    split = P("ta", "ha", "wa", None, None)
    return jax.shard_map(
        per_device,
        mesh=mesh,
        in_specs=(split, split, split, split, P(), P()),
        out_specs=(split, split, split),
        check_vma=False,
    )
```

```python
import functools
import math

import jax
import jax.numpy as jnp
import numpy as np
from jax import lax
from jax.experimental import pallas as pl
from jax.experimental.pallas import tpu as pltpu
from jax.sharding import PartitionSpec as P


NEG = -1e30
LOG2E = 1.4426950408889634
EVEN, ODD = 1000, 1001
AXES = ("ta", "ha", "wa")


def matchings(n):
    even = [(i, i ^ 1) for i in range(n) if (i ^ 1) < n]
    odd = [(i, ((i + 1) ^ 1) - 1) for i in range(n) if 0 <= ((i + 1) ^ 1) - 1 < n]
    return [m for m in (even, odd) if m]


def swap(axis, sends):
    got = []
    for k, pairs in enumerate(matchings(lax.axis_size(axis))):
        got.append(lax.ppermute(sends[k], axis, pairs))
    return got


def sent_layer(axis, k, length):
    odd = lax.rem(lax.axis_index(axis), 2)
    return (1 - odd if k == 0 else odd) * (length - 1)


def by_parity(axis, count, length, put):
    odd = lax.rem(lax.axis_index(axis), 2)

    @pl.when(odd == 0)
    def _():
        for k in range(count):
            put(k, length - 1 if k == 0 else 0)

    @pl.when(odd == 1)
    def _():
        for k in range(count):
            put(k, 0 if k == 0 else length - 1)


def prepare_kernel(block, count, *refs):
    T, H, W, C = block
    args, refs = refs[:4], refs[4:]
    faces, wholes, (buf, sems) = refs[: 2 * count], refs[2 * count : 2 * count + 2], refs[-2:]
    copies = [
        [pltpu.make_async_copy(args[a].at[t], buf.at[a, t], sems.at[a, t]) for t in range(T)]
        for a in range(4)
    ]
    for a in range(4):
        for copy in copies[a]:
            copy.start()
    width = buf.shape[-1]
    for a in range(4):
        for copy in copies[a]:
            copy.wait()
        whole = wholes[a // 2]
        for k in range(count):
            layer = sent_layer("ha", k, H)
            out = faces[(a // 2) * count + k]
            for w in range(W):
                out[a % 2, w * T * C : (w + 1) * T * C, :] = buf[a, :, layer, w].reshape(
                    T * C, width
                )
        for w in range(W):
            for t in range(T):
                r = (w * T + t) * H * C
                whole[a % 2, r : r + H * C, :] = buf[a, t, :, w].reshape(H * C, width)


def time_kernel(block, near, count, own_ref, *refs):
    T, H, W, C = block
    ha, outs = refs[:near], refs[near:]

    def put(k, t):
        for a in range(own_ref.shape[0]):
            for w in range(W):
                i = w * T + t
                parts = [own_ref[a, i * H * C : (i + 1) * H * C, :]]
                parts += [r[a, i * C : (i + 1) * C, :] for r in ha]
                n = (H + near) * C
                outs[k][a, w * n : (w + 1) * n, :] = jnp.concatenate(parts, axis=0)

    by_parity("ta", count, T, put)


def column_kernel(block, count, *refs):
    _, _, W, _ = block
    pieces, outs = refs[: len(refs) - count], refs[len(refs) - count :]

    def put(k, w):
        for a in range(outs[k].shape[0]):
            at = 0
            for r in pieces:
                n = r.shape[1] // W
                outs[k][a, at : at + n, :] = r[a, w * n : (w + 1) * n, :]
                at += n

    by_parity("wa", count, W, put)


def local(kernel, out_shape, operands, space=pltpu.VMEM, **kw):
    place = pl.BlockSpec(memory_space=space)
    return pl.pallas_call(
        kernel,
        out_shape=out_shape,
        in_specs=[place] * len(operands),
        out_specs=[pl.BlockSpec(memory_space=pltpu.VMEM)] * len(out_shape),
        compiler_params=pltpu.CompilerParams(vmem_limit_bytes=16 << 20),
        **kw,
    )(*operands)


def spread(own, ha, block, counts, name):
    _, H, W, C = block
    k, _, width = own.shape
    kind = pltpu.VMEM
    n = W * (H + counts[1]) * C
    ta = swap(
        "ta",
        local(
            functools.partial(time_kernel, block, counts[1], counts[0]),
            [kind((k, n, width), own.dtype)] * counts[0],
            [own] + ha,
            name=name + "_time",
        ),
    )
    n = sum(p.shape[1] for p in [own] + ha + ta) // W
    wa = swap(
        "wa",
        local(
            functools.partial(column_kernel, block, counts[2]),
            [kind((k, n, width), own.dtype)] * counts[2],
            [own] + ha + ta,
            name=name + "_column",
        ),
    )
    return ha + ta + wa


def stat_halo(own, block):
    T, H, W, C = block
    k, _, width = own.shape

    def exchange(axis, first, last):
        odd = lax.rem(lax.axis_index(axis), 2) == 1
        return swap(axis, [jnp.where(odd, first, last), jnp.where(odd, last, first)])

    grid = own.reshape(k, W, T, H, C, width)
    ha = exchange(
        "ha",
        grid[:, :, :, 0].reshape(k, W * T * C, width),
        grid[:, :, :, H - 1].reshape(k, W * T * C, width),
    )
    own_t = own.reshape(k, W, T, H * C, width)
    ha_t = [p.reshape(k, W, T, C, width) for p in ha]

    def time_layer(t):
        layers = [own_t[:, :, t]] + [p[:, :, t] for p in ha_t]
        return jnp.concatenate(layers, axis=2).reshape(k, -1, width)

    ta = exchange("ta", time_layer(0), time_layer(T - 1))

    def column(w):
        return jnp.concatenate(
            [p.reshape(k, W, -1, width)[:, w] for p in [own] + ha + ta], axis=1
        )

    return ha + ta + exchange("wa", column(0), column(W - 1))


def piece_coords(block, counts):
    T, H, W, C = block
    marks = (EVEN, ODD)

    own = [[[(t, h, w) for h in range(H)] for t in range(T)] for w in range(W)]
    pieces = [np.array(own, np.int32).reshape(W, -1, 3)]
    for m in marks[: counts[1]]:
        pieces.append(np.array([[(t, m, w) for t in range(T)] for w in range(W)], np.int32))
    hs = list(range(H)) + list(marks[: counts[1]])
    for m in marks[: counts[0]]:
        pieces.append(np.array([[(m, h, w) for h in hs] for w in range(W)], np.int32))
    column = np.concatenate([p[0] for p in pieces], axis=0)
    out = [p.reshape(-1, 3) for p in pieces]
    for m in marks[: counts[2]]:
        c = column.copy()
        c[:, 2] = m
        out.append(c)
    return np.repeat(np.concatenate(out, axis=0), C, axis=0)


def codes_kernel(block, grids, *refs):
    sources, outs, bufs, sems = refs[:4], refs[4:7], refs[7:11], refs[11]
    copies = [pltpu.make_async_copy(s, b, sems.at[i]) for i, (s, b) in enumerate(zip(sources, bufs))]
    for copy in copies:
        copy.start()
    for copy in copies:
        copy.wait()
    oc_ref, kc_ref, valid_ref, radius_ref = bufs
    query_ref, key_ref, closed_ref = outs
    r = radius_ref[...]
    closed = 8 + (1 - r[0:1]) + 2 * (1 - r[1:2]) + 4 * (1 - r[2:3])
    closed_ref[...] = jnp.broadcast_to(closed, closed_ref.shape)
    code = same = 0
    bad_key = bad_own = 0
    for a, axis in enumerate(AXES):
        length, grid = block[a], grids[a]

        def line(i):
            i = i % grid
            if a == 0:
                return valid_ref[i, 1:2, 1:2]
            if a == 1:
                return valid_ref[1, 1:2, i : i + 1]
            return valid_ref[1, i : i + 1, 1:2]

        low = 1 - line(0)
        high = grid - 3 + line(-1) + line(-2)
        index = lax.axis_index(axis)
        odd = lax.rem(index, 2)
        at_even = jnp.where(odd == 1, -1, length)
        at_odd = jnp.where(odd == 1, length, -1)
        own = oc_ref[:, a : a + 1]
        outer = kc_ref[a : a + 1, :]
        outer = jnp.where(outer == EVEN, at_even, jnp.where(outer == ODD, at_odd, outer))
        place = outer + index * length
        here = own + index * length
        outside = jnp.where((place >= 0) & (place < grid), 0, 8)
        apart = jnp.abs(own - outer)
        same = same | apart
        code = code | jnp.where(apart > 1, 8, apart << a) | outside
        bad_key = bad_key | jnp.where((place >= low) & (place <= high), 0, 8)
        bad_own = bad_own | jnp.where((here >= low) & (here <= high), 0, 8)
    query_ref[...] = code | jnp.where(same == 0, 0, bad_key)
    key_ref[...] = code | jnp.where(same == 0, 0, bad_own)


NT = (((1,), (1,)), ((), ()))
NN = (((1,), (0,)), ((), ()))


def dot(a, b, dims):
    return lax.dot_general(a, b, dims, preferred_element_type=jnp.float32)


def gather(refs, which, cols, pad):
    parts = [r[which, :, cols] for r in refs]
    if pad:
        parts.append(jnp.zeros((pad, parts[0].shape[1]), parts[0].dtype))
    return jnp.concatenate(parts, axis=0)


def put_tiles(ref, value, cols):
    T, H, W, C, _ = ref.shape
    value = value.astype(ref.dtype)
    for w in range(W):
        for t in range(T):
            r = (w * T + t) * H * C
            ref[t, :, w, :, cols] = value[r : r + H * C].reshape(H, C, value.shape[1])


def query_kernel(cfg, closed_ref, code_ref, qd_ref, *rest):
    heads, depth, pad, count = cfg
    kv = rest[:count]
    dq_ref, stat_ref, s_ref, g_ref, d_ref = rest[count:]
    scale = 1.0 / math.sqrt(depth)
    rows = qd_ref.shape[1]
    step = math.gcd(rows, 32)
    stat_ref[...] = jnp.zeros(stat_ref.shape, jnp.float32)

    def columns(h):
        return slice(h * depth, (h + 1) * depth)

    def products(h):
        cols = columns(h)
        s_ref[h % 2] = dot(qd_ref[0, :, cols], gather(kv, 0, cols, pad), NT)
        g_ref[h % 2] = dot(qd_ref[1, :, cols], gather(kv, 1, cols, pad), NT)

    products(0)
    for h in range(heads):
        if h + 1 < heads:
            products(h + 1)
        ratios = []
        for r in range(0, rows, step):
            band = slice(r, r + step)
            allowed = (code_ref[band, :] & closed_ref[0:1, h : h + 1]) == 0
            scores = jnp.where(allowed, s_ref[h % 2, band, :], NEG)
            peak = jnp.max(scores, axis=1, keepdims=True)
            raised = jnp.exp2((scores - peak) * (scale * LOG2E))
            total = jnp.sum(raised, axis=1, keepdims=True)
            grads = g_ref[h % 2, band, :]
            drift = jnp.sum(raised * grads, axis=1, keepdims=True) / total
            d_ref[h % 2, band, :] = (raised * (grads - drift)).astype(jnp.bfloat16)
            stat_ref[band, h : h + 1] = peak * (scale * LOG2E) + jnp.log2(total)
            stat_ref[band, heads + h : heads + h + 1] = drift
            ratios.append(scale / total)
        cols = columns(h)
        product = dot(d_ref[h % 2], gather(kv, 0, cols, pad), NN)
        put_tiles(dq_ref, product * jnp.concatenate(ratios, axis=0), cols)


def key_kernel(cfg, closed_ref, code_ref, kv_ref, *rest):
    heads, depth, pad, count = cfg
    qd = rest[:count]
    st = rest[count : 2 * count]
    dk_ref, dv_ref, row_ref = rest[2 * count :]
    scale = 1.0 / math.sqrt(depth)
    parts = [r[0] for r in st]
    if pad:
        parts.append(jnp.zeros((pad, parts[0].shape[1]), jnp.float32))
    row_ref[...] = jnp.concatenate(parts, axis=0).T
    for h in range(heads):
        cols = slice(h * depth, (h + 1) * depth)
        queries = gather(qd, 0, cols, pad)
        cotangent = gather(qd, 1, cols, pad)
        allowed = (code_ref[...] & closed_ref[0:1, h : h + 1]) == 0
        scores = dot(kv_ref[0, :, cols], queries, NT) * (scale * LOG2E)
        scores = jnp.where(allowed, scores, NEG)
        attention = jnp.exp2(scores - row_ref[h : h + 1, :])
        grads = dot(kv_ref[1, :, cols], cotangent, NT)
        score_grads = (attention * (grads - row_ref[heads + h : heads + h + 1, :])).astype(
            jnp.bfloat16
        )
        put_tiles(dk_ref, dot(score_grads, queries, NN) * scale, cols)
        put_tiles(dv_ref, dot(attention.astype(jnp.bfloat16), cotangent, NN), cols)


def per_device(queries, key_states, value_states, output_cotangent, tile_valid, window_radius):
    T, H, W, C, width = queries.shape
    block = (T, H, W, C)
    heads = window_radius.shape[0]
    depth = width // heads
    sizes = tuple(lax.axis_size(a) for a in AXES)
    grids = tuple(n * b for n, b in zip(sizes, block))
    counts = tuple(len(matchings(n)) for n in sizes)
    rows = T * H * W * C

    kind = jax.ShapeDtypeStruct
    args = [
        pltpu.with_memory_space_constraint(x, pltpu.HBM)
        for x in (key_states, value_states, queries, output_cotangent)
    ]
    made = local(
        functools.partial(prepare_kernel, block, counts[1]),
        [pltpu.VMEM((2, W * T * C, width), jnp.bfloat16)] * (2 * counts[1])
        + [pltpu.VMEM((2, rows, width), jnp.bfloat16)] * 2,
        args,
        space=pltpu.HBM,
        scratch_shapes=[
            pltpu.VMEM((4, T, H, W, C, width), jnp.bfloat16),
            pltpu.SemaphoreType.DMA((4, T)),
        ],
        name="prepare",
    )
    kv, qd = made[-2:]
    kv_ha = swap("ha", made[: counts[1]])
    qd_ha = swap("ha", made[counts[1] : 2 * counts[1]])
    kv_pieces = [kv] + spread(kv, kv_ha, block, counts, "kv")
    qd_pieces = [qd] + spread(qd, qd_ha, block, counts, "qd")

    coords = piece_coords(block, counts)
    total = coords.shape[0]
    padded = -(-total // 128) * 128
    pad = padded - total
    outer = np.full((8, padded), -(1 << 20), np.int32)
    outer[:3, :total] = coords.T
    inner = np.zeros((rows, 8), np.int32)
    inner[:, :3] = coords[:rows]
    cfg = (heads, depth, pad, len(kv_pieces))
    native = kind(queries.shape, jnp.bfloat16)
    lanes = -(-2 * heads // 128) * 128
    tables = [inner, outer, tile_valid.transpose(0, 2, 1), window_radius.T]
    query_code, key_code, closed = local(
        functools.partial(codes_kernel, block, grids),
        [pltpu.VMEM((rows, padded), jnp.int32)] * 2 + [pltpu.VMEM((8, heads), jnp.int32)],
        [pltpu.with_memory_space_constraint(jnp.asarray(x), pltpu.HBM) for x in tables],
        space=pltpu.HBM,
        scratch_shapes=[pltpu.VMEM(x.shape, jnp.int32) for x in tables]
        + [pltpu.SemaphoreType.DMA((4,))],
        name="codes",
    )

    query_gradient, stats = local(
        functools.partial(query_kernel, cfg),
        [native, pltpu.VMEM((rows, lanes), jnp.float32)],
        [closed, query_code, qd] + kv_pieces,
        scratch_shapes=[pltpu.VMEM((2, rows, padded), jnp.float32)] * 2
        + [pltpu.VMEM((2, rows, padded), jnp.bfloat16)],
        name="query_side",
    )
    stat_pieces = [stats[None]] + stat_halo(stats[None], block)
    key_gradient, value_gradient = local(
        functools.partial(key_kernel, cfg),
        [native, native],
        [closed, key_code, kv] + qd_pieces + stat_pieces,
        scratch_shapes=[pltpu.VMEM((lanes, padded), jnp.float32)],
        name="key_side",
    )
    return (query_gradient, key_gradient, value_gradient)


def solution(mesh):
    split = P("ta", "ha", "wa", None, None)

    return jax.shard_map(
        per_device,
        mesh=mesh,
        in_specs=(split, split, split, split, P(), P()),
        out_specs=(split, split, split),
        check_vma=False,
    )
```

```python
import functools
import math

import jax
import jax.numpy as jnp
import numpy as np
from jax import lax
from jax.experimental import pallas as pl
from jax.experimental.pallas import tpu as pltpu
from jax.sharding import PartitionSpec as P


NEG = -1e30
LOG2E = 1.4426950408889634
EVEN, ODD = 1000, 1001
AXES = ("ta", "ha", "wa")


def matchings(n):
    even = [(i, i ^ 1) for i in range(n) if (i ^ 1) < n]
    odd = [(i, ((i + 1) ^ 1) - 1) for i in range(n) if 0 <= ((i + 1) ^ 1) - 1 < n]
    return [m for m in (even, odd) if m]


def swap(axis, sends):
    got = []
    for k, pairs in enumerate(matchings(lax.axis_size(axis))):
        got.append(lax.ppermute(sends[k], axis, pairs))
    return got


def sent_layer(axis, k, length):
    odd = lax.rem(lax.axis_index(axis), 2)
    return (1 - odd if k == 0 else odd) * (length - 1)


def by_parity(axis, count, length, put):
    odd = lax.rem(lax.axis_index(axis), 2)

    @pl.when(odd == 0)
    def _():
        for k in range(count):
            put(k, length - 1 if k == 0 else 0)

    @pl.when(odd == 1)
    def _():
        for k in range(count):
            put(k, 0 if k == 0 else length - 1)


def prepare_kernel(block, axis, count, *refs):
    T, H, W, C = block
    args, faces, (whole, buf, sems) = refs[:2], refs[2 : 2 + count], refs[2 + count :]
    copies = [
        [pltpu.make_async_copy(args[a].at[t], buf.at[a, t], sems.at[a, t]) for t in range(T)]
        for a in range(2)
    ]
    for a in range(2):
        for copy in copies[a]:
            copy.start()
    width = buf.shape[-1]
    for a in range(2):
        for copy in copies[a]:
            copy.wait()
        for w in range(W):
            for t in range(T):
                r = (w * T + t) * H * C
                whole[a, r : r + H * C, :] = buf[a, t, :, w].reshape(H * C, width)
            for k in range(count):
                n = faces[k].shape[1] // W
                if axis == "ha":
                    layer = buf[a, :, sent_layer(axis, k, H), w]
                else:
                    layer = buf[a, sent_layer(axis, k, T), :, w]
                faces[k][a, w * n : (w + 1) * n, :] = layer.reshape(n, width)


def second_kernel(block, axis, near, count, own_ref, *refs):
    T, H, W, C = block
    got, outs = refs[:near], refs[near:]

    def put(k, layer):
        for a in range(own_ref.shape[0]):
            for w in range(W):
                if axis == "ta":
                    r = (w * T + layer) * H * C
                    parts = [own_ref[a, r : r + H * C, :]]
                    at = (w * T + layer) * C
                else:
                    parts = []
                    for t in range(T):
                        r = ((w * T + t) * H + layer) * C
                        parts.append(own_ref[a, r : r + C, :])
                    at = (w * H + layer) * C
                parts += [r[a, at : at + C, :] for r in got]
                n = outs[k].shape[1] // W
                outs[k][a, w * n : (w + 1) * n, :] = jnp.concatenate(parts, axis=0)

    by_parity(axis, count, T if axis == "ta" else H, put)


def column_kernel(block, count, *refs):
    _, _, W, _ = block
    pieces, outs = refs[: len(refs) - count], refs[len(refs) - count :]

    def put(k, w):
        for a in range(outs[k].shape[0]):
            at = 0
            for r in pieces:
                n = r.shape[1] // W
                outs[k][a, at : at + n, :] = r[a, w * n : (w + 1) * n, :]
                at += n

    by_parity("wa", count, W, put)


def local(kernel, out_shape, operands, space=pltpu.VMEM, **kw):
    place = pl.BlockSpec(memory_space=space)
    return pl.pallas_call(
        kernel,
        out_shape=out_shape,
        in_specs=[place] * len(operands),
        out_specs=[pl.BlockSpec(memory_space=pltpu.VMEM)] * len(out_shape),
        compiler_params=pltpu.CompilerParams(vmem_limit_bytes=16 << 20),
        **kw,
    )(*operands)


def spread(own, got, axis, block, counts, name):
    T, H, W, C = block
    k, _, width = own.shape
    near, count, length = (counts[1], counts[0], H) if axis == "ta" else (counts[0], counts[1], T)
    more = swap(
        axis,
        local(
            functools.partial(second_kernel, block, axis, near, count),
            [pltpu.VMEM((k, W * (length + near) * C, width), own.dtype)] * count,
            [own] + got,
            name=name + "_second",
        ),
    )
    columns = []
    for part, pieces in (("near", [own] + got), ("far", more)):
        n = sum(p.shape[1] for p in pieces) // W
        sends = local(
            functools.partial(column_kernel, block, counts[2]),
            [pltpu.VMEM((k, n, width), own.dtype)] * counts[2],
            pieces,
            name=f"{name}_{part}",
        )
        columns += swap("wa", sends)
    return got + more + columns


def piece_coords(block, counts, second):
    T, H, W, C = block
    marks = [(EVEN, ODD)[:n] for n in counts]
    ts, hs = list(range(T)), list(range(H))
    own = [[[(t, h, w) for h in hs] for t in ts] for w in range(W)]
    pieces = [np.array(own, np.int32).reshape(W, -1, 3)]
    if second == "ta":
        for m in marks[1]:
            pieces.append(np.array([[(t, m, w) for t in ts] for w in range(W)], np.int32))
        for m in marks[0]:
            line = hs + list(marks[1])
            pieces.append(np.array([[(m, h, w) for h in line] for w in range(W)], np.int32))
    else:
        for m in marks[0]:
            pieces.append(np.array([[(m, h, w) for h in hs] for w in range(W)], np.int32))
        for m in marks[1]:
            line = ts + list(marks[0])
            pieces.append(np.array([[(t, m, w) for t in line] for w in range(W)], np.int32))
    out = [p.reshape(-1, 3) for p in pieces]
    near = 1 + len(marks[1] if second == "ta" else marks[0])
    for part in (pieces[:near], pieces[near:]):
        for m in marks[2]:
            c = np.concatenate([p[0] for p in part], axis=0)
            c[:, 2] = m
            out.append(c)
    return np.repeat(np.concatenate(out, axis=0), C, axis=0)


def codes_kernel(block, grids, *refs):
    sources, outs, bufs, sems = refs[:5], refs[5:8], refs[8:13], refs[13]
    copies = [pltpu.make_async_copy(s, b, sems.at[i]) for i, (s, b) in enumerate(zip(sources, bufs))]
    for copy in copies:
        copy.start()
    for copy in copies:
        copy.wait()
    oc_ref, kc_ref, qc_ref, valid_ref, radius_ref = bufs
    query_ref, key_ref, closed_ref = outs
    r = radius_ref[...]
    closed = 8 + (1 - r[0:1]) + 2 * (1 - r[1:2]) + 4 * (1 - r[2:3])
    closed_ref[...] = jnp.broadcast_to(closed, closed_ref.shape)
    for outer_ref, code_ref, own_is_key in ((kc_ref, query_ref, False), (qc_ref, key_ref, True)):
        code = same = bad = 0
        for a, axis in enumerate(AXES):
            length, grid = block[a], grids[a]

            def line(i):
                i = i % grid
                if a == 0:
                    return valid_ref[i, 1:2, 1:2]
                if a == 1:
                    return valid_ref[1, 1:2, i : i + 1]
                return valid_ref[1, i : i + 1, 1:2]

            low = 1 - line(0)
            high = grid - 3 + line(-1) + line(-2)
            index = lax.axis_index(axis)
            odd = lax.rem(index, 2)
            at_even = jnp.where(odd == 1, -1, length)
            at_odd = jnp.where(odd == 1, length, -1)
            own = oc_ref[:, a : a + 1]
            outer = outer_ref[a : a + 1, :]
            outer = jnp.where(outer == EVEN, at_even, jnp.where(outer == ODD, at_odd, outer))
            place = outer + index * length
            outside = jnp.where((place >= 0) & (place < grid), 0, 8)
            apart = jnp.abs(own - outer)
            same = same | apart
            code = code | jnp.where(apart > 1, 8, apart << a) | outside
            key = own + index * length if own_is_key else place
            bad = bad | jnp.where((key >= low) & (key <= high), 0, 8)
        code_ref[...] = code | jnp.where(same == 0, 0, bad)


NT = (((1,), (1,)), ((), ()))
NN = (((1,), (0,)), ((), ()))


def dot(a, b, dims):
    return lax.dot_general(a, b, dims, preferred_element_type=jnp.float32)


def gather(refs, which, cols, pad):
    parts = [r[which, :, cols] for r in refs]
    if pad:
        parts.append(jnp.zeros((pad, parts[0].shape[1]), parts[0].dtype))
    return jnp.concatenate(parts, axis=0)


def put_tiles(ref, value, cols):
    T, H, W, C, _ = ref.shape
    value = value.astype(ref.dtype)
    for w in range(W):
        for t in range(T):
            r = (w * T + t) * H * C
            ref[t, :, w, :, cols] = value[r : r + H * C].reshape(H, C, value.shape[1])


def query_kernel(cfg, block, faces, closed_ref, code_ref, qd_ref, *rest):
    heads, depth, pad, count = cfg
    kv = rest[:count]
    dq_ref, stat_ref = rest[count : count + 2]
    first_refs = rest[count + 2 : count + 2 + faces]
    s_ref, g_ref, d_ref = rest[count + 2 + faces :]
    scale = 1.0 / math.sqrt(depth)
    rows = qd_ref.shape[1]
    step = math.gcd(rows, 32)
    stat_ref[...] = jnp.zeros(stat_ref.shape, jnp.float32)

    def columns(h):
        return slice(h * depth, (h + 1) * depth)

    def products(h):
        cols = columns(h)
        s_ref[h % 2] = dot(qd_ref[0, :, cols], gather(kv, 0, cols, pad), NT)
        g_ref[h % 2] = dot(qd_ref[1, :, cols], gather(kv, 1, cols, pad), NT)

    products(0)
    for h in range(heads):
        if h + 1 < heads:
            products(h + 1)
        ratios = []
        for r in range(0, rows, step):
            band = slice(r, r + step)
            allowed = (code_ref[band, :] & closed_ref[0:1, h : h + 1]) == 0
            scores = jnp.where(allowed, s_ref[h % 2, band, :], NEG)
            peak = jnp.max(scores, axis=1, keepdims=True)
            raised = jnp.exp2((scores - peak) * (scale * LOG2E))
            total = jnp.sum(raised, axis=1, keepdims=True)
            grads = g_ref[h % 2, band, :]
            drift = jnp.sum(raised * grads, axis=1, keepdims=True) / total
            d_ref[h % 2, band, :] = (raised * (grads - drift)).astype(jnp.bfloat16)
            stat_ref[0, band, h : h + 1] = peak * (scale * LOG2E) + jnp.log2(total)
            stat_ref[0, band, heads + h : heads + h + 1] = drift
            ratios.append(scale / total)
        cols = columns(h)
        product = dot(d_ref[h % 2], gather(kv, 0, cols, pad), NN)
        put_tiles(dq_ref, product * jnp.concatenate(ratios, axis=0), cols)
    T, H, W, C = block

    def put(k, t):
        for w in range(W):
            r = (w * T + t) * H * C
            first_refs[k][0, w * H * C : (w + 1) * H * C, :] = stat_ref[0, r : r + H * C, :]

    by_parity("ta", faces, T, put)


def key_products_kernel(cfg, begin, closed_ref, code_ref, kv_ref, *rest):
    _, depth, pad, count = cfg
    qd, (s_ref, g_ref) = rest[:count], rest[count:]
    scale = 1.0 / math.sqrt(depth)
    for i in range(s_ref.shape[0]):
        h = begin + i
        cols = slice(h * depth, (h + 1) * depth)
        allowed = (code_ref[...] & closed_ref[0:1, h : h + 1]) == 0
        scores = dot(kv_ref[0, :, cols], gather(qd, 0, cols, pad), NT) * (scale * LOG2E)
        s_ref[i] = jnp.where(allowed, scores, NEG)
        g_ref[i] = dot(kv_ref[1, :, cols], gather(qd, 1, cols, pad), NT)


def key_kernel(cfg, parts, *refs):
    heads, depth, pad, count = cfg
    products, refs = refs[: 2 * parts], refs[2 * parts :]
    qd, st = refs[:count], refs[count : 2 * count]
    dk_ref, dv_ref, row_ref = refs[2 * count :]
    scale = 1.0 / math.sqrt(depth)
    lines = [r[0] for r in st]
    if pad:
        lines.append(jnp.zeros((pad, lines[0].shape[1]), jnp.float32))
    row_ref[...] = jnp.concatenate(lines, axis=0).T
    each = heads // parts
    for h in range(heads):
        cols = slice(h * depth, (h + 1) * depth)
        s_ref, g_ref = products[2 * (h // each) : 2 * (h // each) + 2]
        attention = jnp.exp2(s_ref[h % each] - row_ref[h : h + 1, :])
        drift = row_ref[heads + h : heads + h + 1, :]
        score_grads = (attention * (g_ref[h % each] - drift)).astype(jnp.bfloat16)
        put_tiles(dk_ref, dot(score_grads, gather(qd, 0, cols, pad), NN) * scale, cols)
        put_tiles(dv_ref, dot(attention.astype(jnp.bfloat16), gather(qd, 1, cols, pad), NN), cols)


def per_device(queries, key_states, value_states, output_cotangent, tile_valid, window_radius):
    T, H, W, C, width = queries.shape
    block = (T, H, W, C)
    heads = window_radius.shape[0]
    depth = width // heads
    sizes = tuple(lax.axis_size(a) for a in AXES)
    grids = tuple(n * b for n, b in zip(sizes, block))
    counts = tuple(len(matchings(n)) for n in sizes)
    rows = T * H * W * C

    kind = jax.ShapeDtypeStruct
    args = [
        pltpu.with_memory_space_constraint(x, pltpu.HBM)
        for x in (key_states, value_states, queries, output_cotangent)
    ]

    def prepared(pair, axis, name):
        a = AXES.index(axis)
        n = W * C * (T if axis == "ha" else H)
        made = local(
            functools.partial(prepare_kernel, block, axis, counts[a]),
            [pltpu.VMEM((2, n, width), jnp.bfloat16)] * counts[a]
            + [pltpu.VMEM((2, rows, width), jnp.bfloat16)],
            pair,
            space=pltpu.HBM,
            scratch_shapes=[
                pltpu.VMEM((2, T, H, W, C, width), jnp.bfloat16),
                pltpu.SemaphoreType.DMA((2, T)),
            ],
            name=name + "_prepare",
        )
        return made[-1], swap(axis, made[:-1])

    kv, kv_ha = prepared(args[:2], "ha", "kv")
    qd, qd_ta = prepared(args[2:], "ta", "qd")
    kv_pieces = [kv] + spread(kv, kv_ha, "ta", block, counts, "kv")
    qd_pieces = [qd] + spread(qd, qd_ta, "ha", block, counts, "qd")

    def table(second):
        coords = piece_coords(block, counts, second)
        total = coords.shape[0]
        padded = -(-total // 128) * 128
        out = np.full((8, padded), -(1 << 20), np.int32)
        out[:3, :total] = coords.T
        inner = np.zeros((rows, 8), np.int32)
        inner[:, :3] = coords[:rows]
        return inner, out, padded - total

    inner, outer_k, pad_k = table("ta")
    _, outer_q, pad_q = table("ha")
    kcfg = (heads, depth, pad_k, len(kv_pieces))
    qcfg = (heads, depth, pad_q, len(qd_pieces))
    wide_k, wide_q = outer_k.shape[1], outer_q.shape[1]
    native = kind(queries.shape, jnp.bfloat16)
    lanes = -(-2 * heads // 128) * 128
    tables = [inner, outer_k, outer_q, tile_valid.transpose(0, 2, 1), window_radius.T]
    query_code, key_code, closed = local(
        functools.partial(codes_kernel, block, grids),
        [
            pltpu.VMEM((rows, wide_k), jnp.int32),
            pltpu.VMEM((rows, wide_q), jnp.int32),
            pltpu.VMEM((8, heads), jnp.int32),
        ],
        [pltpu.with_memory_space_constraint(jnp.asarray(x), pltpu.HBM) for x in tables],
        space=pltpu.HBM,
        scratch_shapes=[pltpu.VMEM(x.shape, jnp.int32) for x in tables]
        + [pltpu.SemaphoreType.DMA((len(tables),))],
        name="codes",
    )

    made = local(
        functools.partial(query_kernel, kcfg, block, counts[0]),
        [native, pltpu.VMEM((1, rows, lanes), jnp.float32)]
        + [pltpu.VMEM((1, W * H * C, lanes), jnp.float32)] * counts[0],
        [closed, query_code, qd] + kv_pieces,
        scratch_shapes=[pltpu.VMEM((2, rows, wide_k), jnp.float32)] * 2
        + [pltpu.VMEM((2, rows, wide_k), jnp.bfloat16)],
        name="query_side",
    )
    query_gradient, stats = made[:2]
    st_ta = swap("ta", made[2:])
    stat_pieces = [stats] + spread(stats, st_ta, "ha", block, counts, "st")
    parts = math.gcd(heads, 2)
    products = []
    for i in range(parts):
        products += local(
            functools.partial(key_products_kernel, qcfg, i * heads // parts),
            [pltpu.VMEM((heads // parts, rows, wide_q), jnp.float32)] * 2,
            [closed, key_code, kv] + qd_pieces,
            name=f"key_products_{i}",
        )
    key_gradient, value_gradient = local(
        functools.partial(key_kernel, qcfg, parts),
        [native, native],
        products + qd_pieces + stat_pieces,
        scratch_shapes=[pltpu.VMEM((lanes, wide_q), jnp.float32)],
        name="key_side",
    )
    return (query_gradient, key_gradient, value_gradient)


def solution(mesh):
    split = P("ta", "ha", "wa", None, None)

    return jax.shard_map(
        per_device,
        mesh=mesh,
        in_specs=(split, split, split, split, P(), P()),
        out_specs=(split, split, split),
        check_vma=False,
    )
```

```python
import functools
import math

import jax
import jax.numpy as jnp
import numpy as np
from jax import lax
from jax.experimental import pallas as pl
from jax.experimental.pallas import tpu as pltpu
from jax.sharding import PartitionSpec as P


NEG = -1e30
LOG2E = 1.4426950408889634
EVEN, ODD = 1000, 1001
AXES = ("ta", "ha", "wa")


def matchings(axis):
    n, m = lax.axis_size(axis), lax.axis_size("wa")
    if axis == "wa":
        sets = [[(i, i + 1) for i in range(k, n - 1, 2)] for k in range(2)]
        return [s + [(j, i) for i, j in s] for s in sets if s]
    sets = []
    for k in range(min(2, n - 1)):
        paired = [(i, i + 1) for i in range(k, n - 1, 2)]
        alone = sorted(set(range(n)) - {i for p in paired for i in p})
        pairs = [(i * m + w, j * m + w) for w in range(m) for i, j in paired]
        pairs += [(i * m + w, i * m + w + 1) for i in alone for w in range(0, m - 1, 2)]
        sets.append(pairs + [(j, i) for i, j in pairs])
    return sets


def swap(axis, sends):
    axes = axis if axis == "wa" else (axis, "wa")
    got = []
    for k, pairs in enumerate(matchings(axis)):
        got.append(lax.ppermute(sends[k], axes, pairs))
    return got


def sent_layer(axis, k, length):
    odd = lax.rem(lax.axis_index(axis), 2)
    return (1 - odd if k == 0 else odd) * (length - 1)


def by_parity(axis, count, length, put):
    odd = lax.rem(lax.axis_index(axis), 2)

    @pl.when(odd == 0)
    def _():
        for k in range(count):
            put(k, length - 1 if k == 0 else 0)

    @pl.when(odd == 1)
    def _():
        for k in range(count):
            put(k, 0 if k == 0 else length - 1)


def prepare_kernel(block, plan, *refs):
    T, H, W, C = block
    count = len(plan)
    args, faces, (whole, buf, sems) = refs[:2], refs[2 : 2 + count], refs[2 + count :]
    copies = [
        [pltpu.make_async_copy(args[a].at[t], buf.at[a, t], sems.at[a, t]) for t in range(T)]
        for a in range(2)
    ]
    for a in range(2):
        for copy in copies[a]:
            copy.start()
    width = buf.shape[-1]
    for a in range(2):
        for copy in copies[a]:
            copy.wait()
        for w in range(W):
            for t in range(T):
                r = (w * T + t) * H * C
                whole[a, r : r + H * C, :] = buf[a, t, :, w].reshape(H * C, width)
            for face, (axis, k) in zip(faces, plan):
                n = face.shape[1] // W
                if axis == "ha":
                    layer = buf[a, :, sent_layer(axis, k, H), w]
                else:
                    layer = buf[a, sent_layer(axis, k, T), :, w]
                face[a, w * n : (w + 1) * n, :] = layer.reshape(n, width)


def corner_kernel(block, near, count, *refs):
    T, _, W, C = block
    got, outs = refs[:near], refs[near:]

    def put(k, t):
        for a in range(got[0].shape[0]):
            for w in range(W):
                at = (w * T + t) * C
                outs[k][a, w * near * C : (w + 1) * near * C, :] = jnp.concatenate(
                    [r[a, at : at + C, :] for r in got], axis=0
                )

    by_parity("ta", count, T, put)


def second_kernel(block, axis, near, count, own_ref, *refs):
    T, H, W, C = block
    got, outs = refs[:near], refs[near:]

    def put(k, layer):
        for a in range(own_ref.shape[0]):
            for w in range(W):
                if axis == "ta":
                    r = (w * T + layer) * H * C
                    parts = [own_ref[a, r : r + H * C, :]]
                    at = (w * T + layer) * C
                else:
                    parts = []
                    for t in range(T):
                        r = ((w * T + t) * H + layer) * C
                        parts.append(own_ref[a, r : r + C, :])
                    at = (w * H + layer) * C
                parts += [r[a, at : at + C, :] for r in got]
                n = outs[k].shape[1] // W
                outs[k][a, w * n : (w + 1) * n, :] = jnp.concatenate(parts, axis=0)

    by_parity(axis, count, T if axis == "ta" else H, put)


def column_kernel(block, count, *refs):
    _, _, W, _ = block
    pieces, outs = refs[: len(refs) - count], refs[len(refs) - count :]

    def put(k, w):
        for a in range(outs[k].shape[0]):
            at = 0
            for r in pieces:
                n = r.shape[1] // W
                outs[k][a, at : at + n, :] = r[a, w * n : (w + 1) * n, :]
                at += n

    by_parity("wa", count, W, put)


def local(kernel, out_shape, operands, space=pltpu.VMEM, **kw):
    place = pl.BlockSpec(memory_space=space)
    made = pl.pallas_call(
        kernel,
        out_shape=out_shape,
        in_specs=[place] * len(operands),
        out_specs=[pl.BlockSpec(memory_space=pltpu.VMEM)] * len(out_shape),
        compiler_params=pltpu.CompilerParams(vmem_limit_bytes=16 << 20),
        **kw,
    )(*operands)
    return list(made)


def column_swap(pieces, block, counts, name):
    k, _, width = pieces[0].shape
    n = sum(p.shape[1] for p in pieces) // block[2]
    sends = local(
        functools.partial(column_kernel, block, counts[2]),
        [pltpu.VMEM((k, n, width), pieces[0].dtype)] * counts[2],
        pieces,
        name=name,
    )
    return swap("wa", sends)


def spread(own, got, block, counts, name):
    T, _, W, C = block
    k, _, width = own.shape
    more = swap(
        "ha",
        local(
            functools.partial(second_kernel, block, "ha", counts[0], counts[1]),
            [pltpu.VMEM((k, W * (T + counts[0]) * C, width), own.dtype)] * counts[1],
            [own] + got,
            name=name + "_second",
        ),
    )
    near = column_swap([own] + got, block, counts, name + "_near")
    far = column_swap(more, block, counts, name + "_far")
    return got + more + near + far


def spread_early(own, ha, ta, block, counts, name):
    _, _, W, C = block
    k, _, width = own.shape
    corners = swap(
        "ta",
        local(
            functools.partial(corner_kernel, block, counts[1], counts[0]),
            [pltpu.VMEM((k, W * counts[1] * C, width), own.dtype)] * counts[0],
            ha,
            name=name + "_corner",
        ),
    )
    near = [own] + ha + ta
    near += column_swap(near, block, counts, name + "_near")
    far = corners + column_swap(corners, block, counts, name + "_far")
    return near, far


def piece_coords(block, counts, early):
    T, H, W, C = block
    marks = [(EVEN, ODD)[:n] for n in counts]
    ts, hs, ws = list(range(T)), list(range(H)), list(range(W))

    def piece(cells):
        return np.array([[cell + (w,) for cell in cells] for w in ws], np.int32)

    own = piece([(t, h) for t in ts for h in hs])
    if early:
        near = [own] + [piece([(t, m) for t in ts]) for m in marks[1]]
        near += [piece([(m, h) for h in hs]) for m in marks[0]]
        far = [piece([(m, h) for h in marks[1]]) for m in marks[0]]
    else:
        near = [own] + [piece([(m, h) for h in hs]) for m in marks[0]]
        far = [piece([(t, m) for t in ts + list(marks[0])]) for m in marks[1]]
    columns = []
    for part in (near, far):
        column = np.concatenate([p[0] for p in part], axis=0)
        columns.append([])
        for m in marks[2]:
            columns[-1].append(column.copy())
            columns[-1][-1][:, 2] = m
    near, far = ([p.reshape(-1, 3) for p in part] for part in (near, far))
    groups = [near + columns[0], far + columns[1]] if early else [near + far + sum(columns, [])]
    return [np.repeat(np.concatenate(g, axis=0), C, axis=0) for g in groups]


def codes_kernel(block, grids, *refs):
    sources, outs, bufs, sems = refs[:5], refs[5:8], refs[8:13], refs[13]
    copies = [pltpu.make_async_copy(s, b, sems.at[i]) for i, (s, b) in enumerate(zip(sources, bufs))]
    for copy in copies:
        copy.start()
    for copy in copies:
        copy.wait()
    oc_ref, kc_ref, qc_ref, valid_ref, radius_ref = bufs
    query_ref, key_ref, closed_ref = outs
    r = radius_ref[...]
    closed = 8 + (1 - r[0:1]) + 2 * (1 - r[1:2]) + 4 * (1 - r[2:3])
    closed_ref[...] = jnp.broadcast_to(closed, closed_ref.shape)
    for outer_ref, code_ref, own_is_key in ((kc_ref, query_ref, False), (qc_ref, key_ref, True)):
        code = same = bad = 0
        for a, axis in enumerate(AXES):
            length, grid = block[a], grids[a]

            def line(i):
                i = i % grid
                if a == 0:
                    return valid_ref[i, 1:2, 1:2]
                if a == 1:
                    return valid_ref[1, 1:2, i : i + 1]
                return valid_ref[1, i : i + 1, 1:2]

            low = 1 - line(0)
            high = grid - 3 + line(-1) + line(-2)
            index = lax.axis_index(axis)
            odd = lax.rem(index, 2)
            at_even = jnp.where(odd == 1, -1, length)
            at_odd = jnp.where(odd == 1, length, -1)
            own = oc_ref[:, a : a + 1]
            outer = outer_ref[a : a + 1, :]
            outer = jnp.where(outer == EVEN, at_even, jnp.where(outer == ODD, at_odd, outer))
            place = outer + index * length
            outside = jnp.where((place >= 0) & (place < grid), 0, 8)
            apart = jnp.abs(own - outer)
            same = same | apart
            code = code | jnp.where(apart > 1, 8, apart << a) | outside
            key = own + index * length if own_is_key else place
            bad = bad | jnp.where((key >= low) & (key <= high), 0, 8)
        code_ref[...] = code | jnp.where(same == 0, 0, bad)


NT = (((1,), (1,)), ((), ()))
NN = (((1,), (0,)), ((), ()))


def dot(a, b, dims):
    return lax.dot_general(a, b, dims, preferred_element_type=jnp.float32)


def gather(groups, which, cols):
    parts = []
    for refs, pad in groups:
        parts += [r[which, :, cols] for r in refs]
        if pad:
            parts.append(jnp.zeros((pad, parts[0].shape[1]), parts[0].dtype))
    return jnp.concatenate(parts, axis=0)


def put_tiles(ref, value, cols):
    T, H, W, C, _ = ref.shape
    value = value.astype(ref.dtype)
    for w in range(W):
        for t in range(T):
            r = (w * T + t) * H * C
            ref[t, :, w, :, cols] = value[r : r + H * C].reshape(H, C, value.shape[1])


def products_kernel(cfg, begin, closed_ref, code_ref, own_ref, *rest):
    depth, pad, count, factor = cfg
    groups, (s_ref, g_ref) = [(rest[:count], pad)], rest[count:]
    wide = s_ref.shape[2]
    for i in range(s_ref.shape[0]):
        h = begin + i
        cols = slice(h * depth, (h + 1) * depth)
        allowed = (code_ref[:, :wide] & closed_ref[0:1, h : h + 1]) == 0
        scores = dot(own_ref[0, :, cols], gather(groups, 0, cols), NT) * factor
        s_ref[i] = jnp.where(allowed, scores, NEG)
        g_ref[i] = dot(own_ref[1, :, cols], gather(groups, 1, cols), NT)


def query_kernel(cfg, block, faces, closed_ref, code_ref, near_s_ref, near_g_ref, qd_ref, *rest):
    heads, depth, pads, counts = cfg
    kv, rest = rest[: sum(counts)], rest[sum(counts) :]
    near, far = (kv[: counts[0]], pads[0]), (kv[counts[0] :], pads[1])
    dq_ref, stat_ref = rest[:2]
    first_refs = rest[2 : 2 + faces]
    s_ref, g_ref, d_ref = rest[2 + faces :]
    scale = 1.0 / math.sqrt(depth)
    rows = qd_ref.shape[1]
    wide = near_s_ref.shape[2]
    step = math.gcd(rows, 32)
    stat_ref[...] = jnp.zeros(stat_ref.shape, jnp.float32)

    def columns(h):
        return slice(h * depth, (h + 1) * depth)

    def products(h):
        cols = columns(h)
        s_ref[h % 2] = dot(qd_ref[0, :, cols], gather([far], 0, cols), NT)
        g_ref[h % 2] = dot(qd_ref[1, :, cols], gather([far], 1, cols), NT)

    products(0)
    for h in range(heads):
        if h + 1 < heads:
            products(h + 1)
        ratios = []
        for r in range(0, rows, step):
            band = slice(r, r + step)
            allowed = (code_ref[band, wide:] & closed_ref[0:1, h : h + 1]) == 0
            scores = jnp.concatenate(
                [near_s_ref[h, band, :], jnp.where(allowed, s_ref[h % 2, band, :], NEG)], axis=1
            )
            peak = jnp.max(scores, axis=1, keepdims=True)
            raised = jnp.exp2((scores - peak) * (scale * LOG2E))
            total = jnp.sum(raised, axis=1, keepdims=True)
            grads = jnp.concatenate([near_g_ref[h, band, :], g_ref[h % 2, band, :]], axis=1)
            drift = jnp.sum(raised * grads, axis=1, keepdims=True) / total
            d_ref[h % 2, band, :] = (raised * (grads - drift)).astype(jnp.bfloat16)
            stat_ref[0, band, h : h + 1] = peak * (scale * LOG2E) + jnp.log2(total)
            stat_ref[0, band, heads + h : heads + h + 1] = drift
            ratios.append(scale / total)
        cols = columns(h)
        product = dot(d_ref[h % 2], gather([near, far], 0, cols), NN)
        put_tiles(dq_ref, product * jnp.concatenate(ratios, axis=0), cols)
    T, H, W, C = block

    def put(k, t):
        for w in range(W):
            r = (w * T + t) * H * C
            first_refs[k][0, w * H * C : (w + 1) * H * C, :] = stat_ref[0, r : r + H * C, :]

    by_parity("ta", faces, T, put)


def key_kernel(cfg, parts, *refs):
    heads, depth, pad, count = cfg
    products, refs = refs[: 2 * parts], refs[2 * parts :]
    qd, st = [(refs[:count], pad)], refs[count : 2 * count]
    dk_ref, dv_ref, row_ref = refs[2 * count :]
    scale = 1.0 / math.sqrt(depth)
    lines = [r[0] for r in st]
    if pad:
        lines.append(jnp.zeros((pad, lines[0].shape[1]), jnp.float32))
    row_ref[...] = jnp.concatenate(lines, axis=0).T
    each = heads // parts
    for h in range(heads):
        cols = slice(h * depth, (h + 1) * depth)
        s_ref, g_ref = products[2 * (h // each) : 2 * (h // each) + 2]
        attention = jnp.exp2(s_ref[h % each] - row_ref[h : h + 1, :])
        drift = row_ref[heads + h : heads + h + 1, :]
        score_grads = (attention * (g_ref[h % each] - drift)).astype(jnp.bfloat16)
        put_tiles(dk_ref, dot(score_grads, gather(qd, 0, cols), NN) * scale, cols)
        put_tiles(dv_ref, dot(attention.astype(jnp.bfloat16), gather(qd, 1, cols), NN), cols)


def per_device(queries, key_states, value_states, output_cotangent, tile_valid, window_radius):
    T, H, W, C, width = queries.shape
    block = (T, H, W, C)
    heads = window_radius.shape[0]
    depth = width // heads
    sizes = tuple(lax.axis_size(a) for a in AXES)
    grids = tuple(n * b for n, b in zip(sizes, block))
    counts = tuple(len(matchings(a)) for a in AXES)
    rows = T * H * W * C

    kind = jax.ShapeDtypeStruct
    args = [
        pltpu.with_memory_space_constraint(x, pltpu.HBM)
        for x in (key_states, value_states, queries, output_cotangent)
    ]

    def prepared(pair, axes, name):
        plan = [(x, k) for x in axes for k in range(counts[AXES.index(x)])]
        made = local(
            functools.partial(prepare_kernel, block, plan),
            [pltpu.VMEM((2, W * C * (T if x == "ha" else H), width), jnp.bfloat16) for x, _ in plan]
            + [pltpu.VMEM((2, rows, width), jnp.bfloat16)],
            pair,
            space=pltpu.HBM,
            scratch_shapes=[
                pltpu.VMEM((2, T, H, W, C, width), jnp.bfloat16),
                pltpu.SemaphoreType.DMA((2, T)),
            ],
            name=name + "_prepare",
        )
        got, at = [], 0
        for x in axes:
            n = counts[AXES.index(x)]
            got.append(swap(x, made[at : at + n]))
            at += n
        return made[-1], got

    kv, (kv_ha, kv_ta) = prepared(args[:2], ("ha", "ta"), "kv")
    qd, (qd_ta,) = prepared(args[2:], ("ta",), "qd")
    near, far = spread_early(kv, kv_ha, kv_ta, block, counts, "kv")
    qd_pieces = [qd] + spread(qd, qd_ta, block, counts, "qd")

    def table(early):
        groups = piece_coords(block, counts, early)
        pads = [-len(g) % 128 for g in groups]
        out = np.full((8, sum(len(g) + p for g, p in zip(groups, pads))), -(1 << 20), np.int32)
        at = 0
        for g, p in zip(groups, pads):
            out[:3, at : at + len(g)] = g.T
            at += len(g) + p
        return groups, pads, out

    groups, pads_k, outer_k = table(True)
    _, (pad_q,), outer_q = table(False)
    inner = np.zeros((rows, 8), np.int32)
    inner[:, :3] = groups[0][:rows]
    wide = len(groups[0]) + pads_k[0]
    wide_k, wide_q = outer_k.shape[1], outer_q.shape[1]
    qcfg = (heads, depth, pad_q, len(qd_pieces))
    native = kind(queries.shape, jnp.bfloat16)
    lanes = -(-2 * heads // 128) * 128
    tables = [inner, outer_k, outer_q, tile_valid.transpose(0, 2, 1), window_radius.T]
    query_code, key_code, closed = local(
        functools.partial(codes_kernel, block, grids),
        [
            pltpu.VMEM((rows, wide_k), jnp.int32),
            pltpu.VMEM((rows, wide_q), jnp.int32),
            pltpu.VMEM((8, heads), jnp.int32),
        ],
        [pltpu.with_memory_space_constraint(jnp.asarray(x), pltpu.HBM) for x in tables],
        space=pltpu.HBM,
        scratch_shapes=[pltpu.VMEM(x.shape, jnp.int32) for x in tables]
        + [pltpu.SemaphoreType.DMA((len(tables),))],
        name="codes",
    )

    near_products = local(
        functools.partial(products_kernel, (depth, pads_k[0], len(near), 1.0), 0),
        [pltpu.VMEM((heads, rows, wide), jnp.float32)] * 2,
        [closed, query_code, qd] + near,
        name="query_products",
    )
    kcfg = (heads, depth, pads_k, (len(near), len(far)))
    made = local(
        functools.partial(query_kernel, kcfg, block, counts[0]),
        [native, pltpu.VMEM((1, rows, lanes), jnp.float32)]
        + [pltpu.VMEM((1, W * H * C, lanes), jnp.float32)] * counts[0],
        [closed, query_code] + near_products + [qd] + near + far,
        scratch_shapes=[pltpu.VMEM((2, rows, wide_k - wide), jnp.float32)] * 2
        + [pltpu.VMEM((2, rows, wide_k), jnp.bfloat16)],
        name="query_side",
    )
    query_gradient, stats = made[:2]
    st_ta = swap("ta", made[2:])
    stat_pieces = [stats] + spread(stats, st_ta, block, counts, "st")
    parts = math.gcd(heads, 2)
    products = []
    for i in range(parts):
        products += local(
            functools.partial(
                products_kernel,
                (depth, pad_q, len(qd_pieces), LOG2E / math.sqrt(depth)),
                i * heads // parts,
            ),
            [pltpu.VMEM((heads // parts, rows, wide_q), jnp.float32)] * 2,
            [closed, key_code, kv] + qd_pieces,
            name=f"key_products_{i}",
        )
    key_gradient, value_gradient = local(
        functools.partial(key_kernel, qcfg, parts),
        [native, native],
        products + qd_pieces + stat_pieces,
        scratch_shapes=[pltpu.VMEM((lanes, wide_q), jnp.float32)],
        name="key_side",
    )
    return (query_gradient, key_gradient, value_gradient)


def solution(mesh):
    split = P("ta", "ha", "wa", None, None)

    return jax.shard_map(
        per_device,
        mesh=mesh,
        in_specs=(split, split, split, split, P(), P()),
        out_specs=(split, split, split),
        check_vma=False,
    )
```

```python
import functools
import math

import jax
import jax.numpy as jnp
import numpy as np
from jax import lax
from jax.experimental import pallas as pl
from jax.experimental.pallas import tpu as pltpu
from jax.sharding import PartitionSpec as P


NEG = -1e30
LOG2E = 1.4426950408889634
EVEN, ODD = 1000, 1001
AXES = ("ta", "ha", "wa")


def matchings(axis):
    n, m = lax.axis_size(axis), lax.axis_size("wa")
    if axis == "wa":
        sets = [[(i, i + 1) for i in range(k, n - 1, 2)] for k in range(2)]
        return [s + [(j, i) for i, j in s] for s in sets if s]
    sets = []
    for k in range(min(2, n - 1)):
        paired = [(i, i + 1) for i in range(k, n - 1, 2)]
        alone = sorted(set(range(n)) - {i for p in paired for i in p})
        pairs = [(i * m + w, j * m + w) for w in range(m) for i, j in paired]
        pairs += [(i * m + w, i * m + w + 1) for i in alone for w in range(0, m - 1, 2)]
        sets.append(pairs + [(j, i) for i, j in pairs])
    return sets


def swap(axis, sends):
    axes = axis if axis == "wa" else (axis, "wa")
    got = []
    for k, pairs in enumerate(matchings(axis)):
        got.append(lax.ppermute(sends[k], axes, pairs))
    return got


def sent_layer(axis, k, length):
    odd = lax.rem(lax.axis_index(axis), 2)
    return (1 - odd if k == 0 else odd) * (length - 1)


def by_parity(axis, count, length, put):
    odd = lax.rem(lax.axis_index(axis), 2)

    @pl.when(odd == 0)
    def _():
        for k in range(count):
            put(k, length - 1 if k == 0 else 0)

    @pl.when(odd == 1)
    def _():
        for k in range(count):
            put(k, 0 if k == 0 else length - 1)


def prepare_kernel(block, plan, *refs):
    T, H, W, C = block
    count = len(plan)
    args, faces, (whole, buf, sems) = refs[:2], refs[2 : 2 + count], refs[2 + count :]
    copies = [
        [pltpu.make_async_copy(args[a].at[t], buf.at[a, t], sems.at[a, t]) for t in range(T)]
        for a in range(2)
    ]
    for a in range(2):
        for copy in copies[a]:
            copy.start()
    width = buf.shape[-1]
    for a in range(2):
        for copy in copies[a]:
            copy.wait()
        for w in range(W):
            for t in range(T):
                r = (w * T + t) * H * C
                whole[a, r : r + H * C, :] = buf[a, t, :, w].reshape(H * C, width)
            for face, (axis, k) in zip(faces, plan):
                n = face.shape[1] // W
                if axis == "ha":
                    layer = buf[a, :, sent_layer(axis, k, H), w]
                else:
                    layer = buf[a, sent_layer(axis, k, T), :, w]
                face[a, w * n : (w + 1) * n, :] = layer.reshape(n, width)


def corner_kernel(block, axis, near, count, *refs):
    T, H, W, C = block
    got, outs = refs[:near], refs[near:]
    other = T if axis == "ta" else H

    def put(k, layer):
        for a in range(got[0].shape[0]):
            for w in range(W):
                at = (w * other + layer) * C
                outs[k][a, w * near * C : (w + 1) * near * C, :] = jnp.concatenate(
                    [r[a, at : at + C, :] for r in got], axis=0
                )

    by_parity(axis, count, other, put)


def second_kernel(block, axis, near, count, own_ref, *refs):
    T, H, W, C = block
    got, outs = refs[:near], refs[near:]

    def put(k, layer):
        for a in range(own_ref.shape[0]):
            for w in range(W):
                if axis == "ta":
                    r = (w * T + layer) * H * C
                    parts = [own_ref[a, r : r + H * C, :]]
                    at = (w * T + layer) * C
                else:
                    parts = []
                    for t in range(T):
                        r = ((w * T + t) * H + layer) * C
                        parts.append(own_ref[a, r : r + C, :])
                    at = (w * H + layer) * C
                parts += [r[a, at : at + C, :] for r in got]
                n = outs[k].shape[1] // W
                outs[k][a, w * n : (w + 1) * n, :] = jnp.concatenate(parts, axis=0)

    by_parity(axis, count, T if axis == "ta" else H, put)


def column_kernel(block, count, *refs):
    _, _, W, _ = block
    pieces, outs = refs[: len(refs) - count], refs[len(refs) - count :]

    def put(k, w):
        for a in range(outs[k].shape[0]):
            at = 0
            for r in pieces:
                n = r.shape[1] // W
                outs[k][a, at : at + n, :] = r[a, w * n : (w + 1) * n, :]
                at += n

    by_parity("wa", count, W, put)


def local(kernel, out_shape, operands, space=pltpu.VMEM, out_space=pltpu.VMEM, **kw):
    place = pl.BlockSpec(memory_space=space)
    made = pl.pallas_call(
        kernel,
        out_shape=out_shape,
        in_specs=[place] * len(operands),
        out_specs=[pl.BlockSpec(memory_space=out_space)] * len(out_shape),
        compiler_params=pltpu.CompilerParams(vmem_limit_bytes=16 << 20),
        **kw,
    )(*operands)
    return list(made)


def column_swap(pieces, block, counts, name):
    k, _, width = pieces[0].shape
    n = sum(p.shape[1] for p in pieces) // block[2]
    sends = local(
        functools.partial(column_kernel, block, counts[2]),
        [pltpu.VMEM((k, n, width), pieces[0].dtype)] * counts[2],
        pieces,
        name=name,
    )
    return swap("wa", sends)


def spread(own, got, block, counts, name):
    T, _, W, C = block
    k, _, width = own.shape
    more = swap(
        "ha",
        local(
            functools.partial(second_kernel, block, "ha", counts[0], counts[1]),
            [pltpu.VMEM((k, W * (T + counts[0]) * C, width), own.dtype)] * counts[1],
            [own] + got,
            name=name + "_second",
        ),
    )
    near = column_swap([own] + got, block, counts, name + "_near")
    far = column_swap(more, block, counts, name + "_far")
    return [own], got, near, more, far


def spread_early(own, ha, ta, axis, block, counts, name):
    _, _, W, C = block
    k, _, width = own.shape
    got, near_count, count = (ha, counts[1], counts[0]) if axis == "ta" else (ta, counts[0], counts[1])
    corners = swap(
        axis,
        local(
            functools.partial(corner_kernel, block, axis, near_count, count),
            [pltpu.VMEM((k, W * near_count * C, width), own.dtype)] * count,
            got,
            name=name + "_corner",
        ),
    )
    near = [own] + ha + ta
    near += column_swap(near, block, counts, name + "_near")
    far = corners + column_swap(corners, block, counts, name + "_far")
    return near, far


def piece_coords(block, counts, axis):
    T, H, W, C = block
    marks = [(EVEN, ODD)[:n] for n in counts]
    ts, hs, ws = list(range(T)), list(range(H)), list(range(W))

    def piece(cells):
        return np.array([[cell + (w,) for cell in cells] for w in ws], np.int32)

    near = [piece([(t, h) for t in ts for h in hs])]
    near += [piece([(t, m) for t in ts]) for m in marks[1]]
    near += [piece([(m, h) for h in hs]) for m in marks[0]]
    if axis == "ta":
        far = [piece([(m, h) for h in marks[1]]) for m in marks[0]]
    else:
        far = [piece([(t, m) for t in marks[0]]) for m in marks[1]]
    groups = []
    for part in (near, far):
        column = np.concatenate([p[0] for p in part], axis=0)
        rows = [p.reshape(-1, 3) for p in part]
        for m in marks[2]:
            rows.append(column.copy())
            rows[-1][:, 2] = m
        groups.append(np.repeat(np.concatenate(rows, axis=0), C, axis=0))
    return groups


def codes_kernel(block, grids, own_is_key, *refs):
    sources, (code_ref, closed_ref), bufs, sems = refs[:4], refs[4:6], refs[6:10], refs[10]
    copies = [pltpu.make_async_copy(s, b, sems.at[i]) for i, (s, b) in enumerate(zip(sources, bufs))]
    for copy in copies:
        copy.start()
    for copy in copies:
        copy.wait()
    own_ref, outer_ref, valid_ref, radius_ref = bufs
    r = radius_ref[...]
    closed = 8 + (1 - r[0:1]) + 2 * (1 - r[1:2]) + 4 * (1 - r[2:3])
    closed_ref[...] = jnp.broadcast_to(closed, closed_ref.shape)
    own_all, outer_all = own_ref[...], outer_ref[...]
    if own_is_key:
        own_all = own_all.T
    else:
        outer_all = outer_all.T
    code = same = bad = 0
    for a, axis in enumerate(AXES):
        length, grid = block[a], grids[a]

        def line(i):
            i = i % grid
            if a == 0:
                return valid_ref[i, 1:2, 1:2]
            if a == 1:
                return valid_ref[1, 1:2, i : i + 1]
            return valid_ref[1, i : i + 1, 1:2]

        low = 1 - line(0)
        high = grid - 3 + line(-1) + line(-2)
        index = lax.axis_index(axis)
        odd = lax.rem(index, 2)
        at_even = jnp.where(odd == 1, -1, length)
        at_odd = jnp.where(odd == 1, length, -1)
        if own_is_key:
            own, outer = own_all[:, a : a + 1], outer_all[a : a + 1, :]
        else:
            own, outer = own_all[a : a + 1, :], outer_all[:, a : a + 1]
        outer = jnp.where(outer == EVEN, at_even, jnp.where(outer == ODD, at_odd, outer))
        place = outer + index * length
        outside = jnp.where((place >= 0) & (place < grid), 0, 8)
        apart = jnp.abs(own - outer)
        same = same | apart
        code = code | jnp.where(apart > 1, 8, apart << a) | outside
        key = own + index * length if own_is_key else place
        bad = bad | jnp.where((key >= low) & (key <= high), 0, 8)
    code_ref[...] = code | jnp.where(same == 0, 0, bad)


NT = (((1,), (1,)), ((), ()))
NN = (((1,), (0,)), ((), ()))
TN = (((0,), (0,)), ((), ()))
STEP = 64


def dot(a, b, dims):
    return lax.dot_general(a, b, dims, preferred_element_type=jnp.float32)


def gather(groups, which, cols):
    parts = []
    for refs, pad in groups:
        parts += [r[which, :, cols] for r in refs]
        if pad:
            parts.append(jnp.zeros((pad, parts[0].shape[1]), parts[0].dtype))
    return jnp.concatenate(parts, axis=0)


def put_tiles(ref, value, cols):
    T, H, W, C, _ = ref.shape
    value = value.astype(ref.dtype)
    for w in range(W):
        for t in range(T):
            r = (w * T + t) * H * C
            ref[t, :, w, :, cols] = value[r : r + H * C].reshape(H, C, value.shape[1])


def products_kernel(cfg, closed_ref, code_ref, own_ref, *rest):
    depth, pad, first, own_is_key = cfg
    groups, (s_ref, g_ref) = [(rest[:-2], pad)], rest[-2:]
    factor = LOG2E / math.sqrt(depth)
    for h in range(s_ref.shape[0]):
        cols = slice(h * depth, (h + 1) * depth)
        own, outer = ([own_ref[i, :, cols] for i in (0, 1)], [gather(groups, i, cols) for i in (0, 1)])
        if own_is_key:
            code = code_ref[:, first : first + s_ref.shape[2]]
            scores, grads = (dot(a, b, NT) for a, b in zip(own, outer))
        else:
            code = code_ref[first : first + s_ref.shape[1], :]
            scores, grads = (dot(b, a, NT) for a, b in zip(own, outer))
        s_ref[h] = jnp.where((code & closed_ref[0:1, h : h + 1]) == 0, scores * factor, NEG)
        g_ref[h] = grads


def near_kernel(cfg, closed_ref, code_ref, own_ref, *rest):
    s_ref, g_ref, m_ref = rest[-3:]
    heads, wide, _ = s_ref.shape
    products_kernel(cfg, closed_ref, code_ref, own_ref, *rest[:-1])
    for h in range(heads):
        bands = range(0, wide, STEP)
        peak = functools.reduce(jnp.maximum, [s_ref[h, r : r + STEP, :] for r in bands])
        peak = jnp.max(peak, axis=0, keepdims=True)
        total = part = 0.0
        for r in bands:
            raised = jnp.exp2(s_ref[h, r : r + STEP, :] - peak)
            total = total + raised
            part = part + raised * g_ref[h, r : r + STEP, :]
        m_ref[h, 0:1, :] = peak
        m_ref[h, 1:2, :] = jnp.sum(total, axis=0, keepdims=True)
        m_ref[h, 2:3, :] = jnp.sum(part, axis=0, keepdims=True)


def query_kernel(cfg, block, faces, closed_ref, code_ref, near_s_ref, near_g_ref, near_m_ref, *rest):
    heads, depth, pads, counts = cfg
    qd_ref, rest = rest[0], rest[1:]
    kv, rest = rest[: sum(counts)], rest[sum(counts) :]
    near, far = (kv[: counts[0]], pads[0]), (kv[counts[0] :], pads[1])
    dq_ref, stat_ref = rest[:2]
    first_refs = rest[2 : 2 + faces]
    s_ref, g_ref, d_ref, stat_rows = rest[2 + faces :]
    scale = 1.0 / math.sqrt(depth)
    wide = near_s_ref.shape[1]
    total_rows = code_ref.shape[0]
    stat_rows[...] = jnp.zeros(stat_rows.shape, jnp.float32)

    def columns(h):
        return slice(h * depth, (h + 1) * depth)

    def products(h):
        cols = columns(h)
        scores = dot(gather([far], 0, cols), qd_ref[0, :, cols], NT) * (scale * LOG2E)
        allowed = (code_ref[wide:, :] & closed_ref[0:1, h : h + 1]) == 0
        s_ref[h % 2] = jnp.where(allowed, scores, NEG)
        g_ref[h % 2] = dot(gather([far], 1, cols), qd_ref[1, :, cols], NT)

    products(0)
    for h in range(heads):
        if h + 1 < heads:
            products(h + 1)
        near_peak = near_m_ref[h, 0:1, :]
        scores, grads = s_ref[h % 2], g_ref[h % 2]
        peak = jnp.maximum(near_peak, jnp.max(scores, axis=0, keepdims=True))
        raised = jnp.exp2(scores - peak)
        lower = jnp.exp2(near_peak - peak)
        total = near_m_ref[h, 1:2, :] * lower + jnp.sum(raised, axis=0, keepdims=True)
        part = near_m_ref[h, 2:3, :] * lower + jnp.sum(raised * grads, axis=0, keepdims=True)
        drift = part / total
        logsum = peak + jnp.log2(total)
        stat_rows[h : h + 1, :] = logsum
        stat_rows[heads + h : heads + h + 1, :] = drift
        for r in range(0, total_rows, STEP):
            if r < wide:
                scores, grads = near_s_ref[h, r : r + STEP, :], near_g_ref[h, r : r + STEP, :]
            else:
                at = slice(r - wide, r - wide + STEP)
                scores, grads = s_ref[h % 2, at, :], g_ref[h % 2, at, :]
            attention = jnp.exp2(scores - logsum)
            d_ref[h % 2, r : r + STEP, :] = (attention * (grads - drift)).astype(jnp.bfloat16)
        cols = columns(h)
        put_tiles(dq_ref, dot(d_ref[h % 2], gather([near, far], 0, cols), TN) * scale, cols)
    stat_ref[0] = stat_rows[...].T
    T, H, W, C = block

    def put(k, t):
        for w in range(W):
            r = (w * T + t) * H * C
            first_refs[k][0, w * H * C : (w + 1) * H * C, :] = stat_ref[0, r : r + H * C, :]

    by_parity("ta", faces, T, put)


def statistics_rows(st, pads, block, counts):
    T, H, W, C = block
    na, nh, nw = counts
    own, ta, near = st[0], st[1 : 1 + na], st[1 + na : 1 + na + nw]
    ha, far = st[1 + na + nw : 1 + na + nw + nh], st[1 + na + nw + nh :]
    a, each = T * C, (T + na) * C
    lines = [own[0]]
    lines += [r[0, w * each : w * each + a, :] for r in ha for w in range(W)]
    lines += [r[0] for r in ta]
    cut = T * H * C
    for n, f in zip(near, far):
        lines.append(n[0, :cut, :])
        lines += [f[0, k * each : k * each + a, :] for k in range(nh)]
        lines.append(n[0, cut:, :])
    if pads[0]:
        lines.append(jnp.zeros((pads[0], own.shape[2]), jnp.float32))
    lines += [r[0, w * each + a : (w + 1) * each, :] for r in ha for w in range(W)]
    lines += [f[0, k * each + a : (k + 1) * each, :] for f in far for k in range(nh)]
    if pads[1]:
        lines.append(jnp.zeros((pads[1], own.shape[2]), jnp.float32))
    return jnp.concatenate(lines, axis=0)


def key_kernel(cfg, *refs):
    heads, depth, pads, counts, parts, split, block, axes = cfg
    products, dq_ref, refs = refs[: 2 * parts], refs[2 * parts], refs[2 * parts + 1 :]
    near, far, refs = refs[: counts[0]], refs[counts[0] : sum(counts)], refs[sum(counts) :]
    qd = [(near, pads[0]), (far, pads[1])]
    st, refs = refs[: 1 + 2 * axes[2] + axes[0] + axes[1]], refs[-8:]
    dq_out, dk_out, dv_out, row_ref, dk_ref, dv_ref, dq_sem, sems = refs
    scale = 1.0 / math.sqrt(depth)
    row_ref[...] = statistics_rows(st, pads, block, axes).T
    copies = [pltpu.make_async_copy(dq_ref, dq_out, dq_sem)]
    copies[0].start()
    for h in range(heads):
        cols = slice(h * depth, (h + 1) * depth)
        scores = jnp.concatenate([r[h] for r in products[0::2]], axis=1)
        grads = jnp.concatenate([r[h] for r in products[1::2]], axis=1)
        attention = jnp.exp2(scores - row_ref[h : h + 1, :])
        drift = row_ref[heads + h : heads + h + 1, :]
        score_grads = (attention * (grads - drift)).astype(jnp.bfloat16)
        put_tiles(dk_ref, dot(score_grads, gather(qd, 0, cols), NN) * scale, cols)
        put_tiles(dv_ref, dot(attention.astype(jnp.bfloat16), gather(qd, 1, cols), NN), cols)
        if (h + 1) % (heads // split) == 0:
            i = (h + 1) // (heads // split) - 1
            done = slice((h + 1 - heads // split) * depth, (h + 1) * depth)
            for j, (ref, out) in enumerate(((dk_ref, dk_out), (dv_ref, dv_out))):
                copies.append(
                    pltpu.make_async_copy(
                        ref.at[:, :, :, :, done], out.at[:, :, :, :, done], sems.at[j, i]
                    )
                )
                copies[-1].start()
    for copy in copies:
        copy.wait()


def per_device(queries, key_states, value_states, output_cotangent, tile_valid, window_radius):
    T, H, W, C, width = queries.shape
    block = (T, H, W, C)
    heads = window_radius.shape[0]
    depth = width // heads
    sizes = tuple(lax.axis_size(a) for a in AXES)
    grids = tuple(n * b for n, b in zip(sizes, block))
    counts = tuple(len(matchings(a)) for a in AXES)
    rows = T * H * W * C

    kind = jax.ShapeDtypeStruct
    args = [
        pltpu.with_memory_space_constraint(x, pltpu.HBM)
        for x in (key_states, value_states, queries, output_cotangent)
    ]

    def prepared(pair, axes, name):
        plan = [(x, k) for x in axes for k in range(counts[AXES.index(x)])]
        made = local(
            functools.partial(prepare_kernel, block, plan),
            [pltpu.VMEM((2, W * C * (T if x == "ha" else H), width), jnp.bfloat16) for x, _ in plan]
            + [pltpu.VMEM((2, rows, width), jnp.bfloat16)],
            pair,
            space=pltpu.HBM,
            scratch_shapes=[
                pltpu.VMEM((2, T, H, W, C, width), jnp.bfloat16),
                pltpu.SemaphoreType.DMA((2, T)),
            ],
            name=name + "_prepare",
        )
        got, at = [], 0
        for x in axes:
            n = counts[AXES.index(x)]
            got.append(swap(x, made[at : at + n]))
            at += n
        return made[-1], got

    kv, (kv_ha, kv_ta) = prepared(args[:2], ("ha", "ta"), "kv")
    qd, (qd_ta, qd_ha) = prepared(args[2:], ("ta", "ha"), "qd")
    near, far = spread_early(kv, kv_ha, kv_ta, "ta", block, counts, "kv")
    qd_near, qd_far = spread_early(qd, qd_ha, qd_ta, "ha", block, counts, "qd")

    def table(axis):
        groups = piece_coords(block, counts, axis)
        pads = [-len(g) % 128 for g in groups]
        out = np.full((8, sum(len(g) + p for g, p in zip(groups, pads))), -(1 << 20), np.int32)
        at = 0
        for g, p in zip(groups, pads):
            out[:3, at : at + len(g)] = g.T
            at += len(g) + p
        return groups, pads, out

    groups, pads, outer_k = table("ta")
    _, pads_q, outer_q = table("ha")
    inner = np.zeros((8, rows), np.int32)
    inner[:3] = groups[0][:rows].T
    wide, all_wide = len(groups[0]) + pads[0], outer_k.shape[1]
    native = kind(queries.shape, jnp.bfloat16)
    lanes = -(-2 * heads // 128) * 128

    def codes(outer, own_is_key, name):
        tables = [inner, outer, tile_valid.transpose(0, 2, 1), window_radius.T]
        shape = (rows, all_wide) if own_is_key else (all_wide, rows)
        return local(
            functools.partial(codes_kernel, block, grids, own_is_key),
            [pltpu.VMEM(shape, jnp.int32), pltpu.VMEM((8, heads), jnp.int32)],
            [pltpu.with_memory_space_constraint(jnp.asarray(x), pltpu.HBM) for x in tables],
            space=pltpu.HBM,
            scratch_shapes=[pltpu.VMEM(x.shape, jnp.int32) for x in tables]
            + [pltpu.SemaphoreType.DMA((len(tables),))],
            name=name,
        )

    query_code, closed = codes(outer_k, False, "query_codes")
    key_code, key_closed = codes(outer_q, True, "key_codes")
    near_products = local(
        functools.partial(near_kernel, (depth, pads[0], 0, False)),
        [pltpu.VMEM((heads, wide, rows), jnp.float32)] * 2
        + [pltpu.VMEM((heads, 8, rows), jnp.float32)],
        [closed, query_code, qd] + near,
        name="query_products",
    )
    kcfg = (heads, depth, pads, (len(near), len(far)))
    made = local(
        functools.partial(query_kernel, kcfg, block, counts[0]),
        [pltpu.VMEM(queries.shape, jnp.bfloat16), pltpu.VMEM((1, rows, lanes), jnp.float32)]
        + [pltpu.VMEM((1, W * H * C, lanes), jnp.float32)] * counts[0],
        [closed, query_code] + near_products + [qd] + near + far,
        scratch_shapes=[pltpu.VMEM((2, all_wide - wide, rows), jnp.float32)] * 2
        + [pltpu.VMEM((2, all_wide, rows), jnp.bfloat16), pltpu.VMEM((lanes, rows), jnp.float32)],
        name="query_side",
    )
    query_gradient, stats = made[:2]
    st_ta = swap("ta", made[2:])
    stat_pieces = sum(spread(stats, st_ta, block, counts, "st"), [])
    products = []
    for i, pieces in enumerate((qd_near, qd_far)):
        products += local(
            functools.partial(products_kernel, (depth, pads_q[i], i * wide, True)),
            [pltpu.VMEM((heads, rows, all_wide - wide if i else wide), jnp.float32)] * 2,
            [key_closed, key_code, kv] + pieces,
            name=f"key_products_{i}",
        )
    split = math.gcd(heads, 6)
    lengths = (len(qd_near), len(qd_far))
    query_gradient, key_gradient, value_gradient = local(
        functools.partial(
            key_kernel, (heads, depth, pads_q, lengths, 2, split, block, counts)
        ),
        [native] * 3,
        products + [query_gradient] + qd_near + qd_far + stat_pieces,
        out_space=pltpu.HBM,
        scratch_shapes=[pltpu.VMEM((lanes, all_wide), jnp.float32)]
        + [pltpu.VMEM(queries.shape, jnp.bfloat16)] * 2
        + [pltpu.SemaphoreType.DMA, pltpu.SemaphoreType.DMA((2, split))],
        name="key_side",
    )
    return (query_gradient, key_gradient, value_gradient)


def solution(mesh):
    split = P("ta", "ha", "wa", None, None)

    return jax.shard_map(
        per_device,
        mesh=mesh,
        in_specs=(split, split, split, split, P(), P()),
        out_specs=(split, split, split),
        check_vma=False,
    )
```

```python
import functools
import math

import jax
import jax.numpy as jnp
import numpy as np
from jax import lax
from jax.experimental import pallas as pl
from jax.experimental.pallas import tpu as pltpu
from jax.sharding import PartitionSpec as P


NEG = -1e30
LOG2E = 1.4426950408889634
EVEN, ODD = 1000, 1001
AXES = ("ta", "ha", "wa")


def matchings(axis):
    n, m = lax.axis_size(axis), lax.axis_size("wa")
    if axis == "wa":
        sets = [[(i, i + 1) for i in range(k, n - 1, 2)] for k in range(2)]
        return [s + [(j, i) for i, j in s] for s in sets if s]
    sets = []
    for k in range(min(2, n - 1)):
        paired = [(i, i + 1) for i in range(k, n - 1, 2)]
        alone = sorted(set(range(n)) - {i for p in paired for i in p})
        pairs = [(i * m + w, j * m + w) for w in range(m) for i, j in paired]
        pairs += [(i * m + w, i * m + w + 1) for i in alone for w in range(0, m - 1, 2)]
        sets.append(pairs + [(j, i) for i, j in pairs])
    return sets


def swap(axis, sends):
    axes = axis if axis == "wa" else (axis, "wa")
    got = []
    for k, pairs in enumerate(matchings(axis)):
        got.append(lax.ppermute(sends[k], axes, pairs))
    return got


def sent_layer(axis, k, length):
    odd = lax.rem(lax.axis_index(axis), 2)
    return (1 - odd if k == 0 else odd) * (length - 1)


def by_parity(axis, count, length, put):
    odd = lax.rem(lax.axis_index(axis), 2)

    @pl.when(odd == 0)
    def _():
        for k in range(count):
            put(k, length - 1 if k == 0 else 0)

    @pl.when(odd == 1)
    def _():
        for k in range(count):
            put(k, 0 if k == 0 else length - 1)


def prepare_kernel(block, plan, *refs):
    T, H, W, C = block
    count = len(plan)
    args, faces, (whole, buf, sems) = refs[:2], refs[2 : 2 + count], refs[2 + count :]
    copies = [
        [pltpu.make_async_copy(args[a].at[t], buf.at[a, t], sems.at[a, t]) for t in range(T)]
        for a in range(2)
    ]
    for a in range(2):
        for copy in copies[a]:
            copy.start()
    width = buf.shape[-1]
    for a in range(2):
        for copy in copies[a]:
            copy.wait()
        for w in range(W):
            for t in range(T):
                r = (w * T + t) * H * C
                whole[a, r : r + H * C, :] = buf[a, t, :, w].reshape(H * C, width)
            for face, (axis, k) in zip(faces, plan):
                n = face.shape[1] // W
                if axis == "ha":
                    layer = buf[a, :, sent_layer(axis, k, H), w]
                else:
                    layer = buf[a, sent_layer(axis, k, T), :, w]
                face[a, w * n : (w + 1) * n, :] = layer.reshape(n, width)


def corner_kernel(block, axis, near, count, *refs):
    T, H, W, C = block
    got, outs = refs[:near], refs[near:]
    other = T if axis == "ta" else H

    def put(k, layer):
        for a in range(got[0].shape[0]):
            for w in range(W):
                at = (w * other + layer) * C
                outs[k][a, w * near * C : (w + 1) * near * C, :] = jnp.concatenate(
                    [r[a, at : at + C, :] for r in got], axis=0
                )

    by_parity(axis, count, other, put)


def second_kernel(block, axis, near, count, own_ref, *refs):
    T, H, W, C = block
    got, outs = refs[:near], refs[near:]

    def put(k, layer):
        for a in range(own_ref.shape[0]):
            for w in range(W):
                if axis == "ta":
                    r = (w * T + layer) * H * C
                    parts = [own_ref[a, r : r + H * C, :]]
                    at = (w * T + layer) * C
                else:
                    parts = []
                    for t in range(T):
                        r = ((w * T + t) * H + layer) * C
                        parts.append(own_ref[a, r : r + C, :])
                    at = (w * H + layer) * C
                parts += [r[a, at : at + C, :] for r in got]
                n = outs[k].shape[1] // W
                outs[k][a, w * n : (w + 1) * n, :] = jnp.concatenate(parts, axis=0)

    by_parity(axis, count, T if axis == "ta" else H, put)


def column_kernel(block, count, *refs):
    _, _, W, _ = block
    pieces, outs = refs[: len(refs) - count], refs[len(refs) - count :]

    def put(k, w):
        for a in range(outs[k].shape[0]):
            at = 0
            for r in pieces:
                n = r.shape[1] // W
                outs[k][a, at : at + n, :] = r[a, w * n : (w + 1) * n, :]
                at += n

    by_parity("wa", count, W, put)


def local(kernel, out_shape, operands, space=pltpu.VMEM, out_space=pltpu.VMEM, **kw):
    place = pl.BlockSpec(memory_space=space)
    made = pl.pallas_call(
        kernel,
        out_shape=out_shape,
        in_specs=[place] * len(operands),
        out_specs=[pl.BlockSpec(memory_space=out_space)] * len(out_shape),
        compiler_params=pltpu.CompilerParams(vmem_limit_bytes=16 << 20),
        **kw,
    )(*operands)
    return list(made)


def column_swap(pieces, block, counts, name):
    k, _, width = pieces[0].shape
    n = sum(p.shape[1] for p in pieces) // block[2]
    sends = local(
        functools.partial(column_kernel, block, counts[2]),
        [pltpu.VMEM((k, n, width), pieces[0].dtype)] * counts[2],
        pieces,
        name=name,
    )
    return swap("wa", sends)


def spread(own, got, block, counts, name):
    T, _, W, C = block
    k, _, width = own.shape
    more = swap(
        "ha",
        local(
            functools.partial(second_kernel, block, "ha", counts[0], counts[1]),
            [pltpu.VMEM((k, W * (T + counts[0]) * C, width), own.dtype)] * counts[1],
            [own] + got,
            name=name + "_second",
        ),
    )
    near = column_swap([own] + got, block, counts, name + "_near")
    far = column_swap(more, block, counts, name + "_far")
    return [own], got, near, more, far


def spread_early(own, ha, ta, axis, block, counts, name):
    _, _, W, C = block
    k, _, width = own.shape
    got, near_count, count = (ha, counts[1], counts[0]) if axis == "ta" else (ta, counts[0], counts[1])
    corners = swap(
        axis,
        local(
            functools.partial(corner_kernel, block, axis, near_count, count),
            [pltpu.VMEM((k, W * near_count * C, width), own.dtype)] * count,
            got,
            name=name + "_corner",
        ),
    )
    near = [own] + ha + ta
    near += column_swap(near, block, counts, name + "_near")
    far = corners + column_swap(corners, block, counts, name + "_far")
    return near, far


def piece_coords(block, counts, axis):
    T, H, W, C = block
    marks = [(EVEN, ODD)[:n] for n in counts]
    ts, hs, ws = list(range(T)), list(range(H)), list(range(W))

    def piece(cells):
        return np.array([[cell + (w,) for cell in cells] for w in ws], np.int32)

    near = [piece([(t, h) for t in ts for h in hs])]
    near += [piece([(t, m) for t in ts]) for m in marks[1]]
    near += [piece([(m, h) for h in hs]) for m in marks[0]]
    if axis == "ta":
        far = [piece([(m, h) for h in marks[1]]) for m in marks[0]]
    else:
        far = [piece([(t, m) for t in marks[0]]) for m in marks[1]]
    groups = []
    for part in (near, far):
        column = np.concatenate([p[0] for p in part], axis=0)
        rows = [p.reshape(-1, 3) for p in part]
        for m in marks[2]:
            rows.append(column.copy())
            rows[-1][:, 2] = m
        groups.append(np.repeat(np.concatenate(rows, axis=0), C, axis=0))
    return groups


def codes_kernel(block, grids, own_is_key, *refs):
    sources, (code_ref, closed_ref), bufs, sems = refs[:4], refs[4:6], refs[6:10], refs[10]
    copies = [pltpu.make_async_copy(s, b, sems.at[i]) for i, (s, b) in enumerate(zip(sources, bufs))]
    for copy in copies:
        copy.start()
    for copy in copies:
        copy.wait()
    own_ref, outer_ref, valid_ref, radius_ref = bufs
    r = radius_ref[...]
    closed = 8 + (1 - r[0:1]) + 2 * (1 - r[1:2]) + 4 * (1 - r[2:3])
    closed_ref[...] = jnp.broadcast_to(closed, closed_ref.shape)
    own_all, outer_all = own_ref[...], outer_ref[...]
    if own_is_key:
        own_all = own_all.T
    else:
        outer_all = outer_all.T
    code = same = bad = 0
    for a, axis in enumerate(AXES):
        length, grid = block[a], grids[a]

        def line(i):
            i = i % grid
            if a == 0:
                return valid_ref[i, 1:2, 1:2]
            if a == 1:
                return valid_ref[1, 1:2, i : i + 1]
            return valid_ref[1, i : i + 1, 1:2]

        low = 1 - line(0)
        high = grid - 3 + line(-1) + line(-2)
        index = lax.axis_index(axis)
        odd = lax.rem(index, 2)
        at_even = jnp.where(odd == 1, -1, length)
        at_odd = jnp.where(odd == 1, length, -1)
        if own_is_key:
            own, outer = own_all[:, a : a + 1], outer_all[a : a + 1, :]
        else:
            own, outer = own_all[a : a + 1, :], outer_all[:, a : a + 1]
        outer = jnp.where(outer == EVEN, at_even, jnp.where(outer == ODD, at_odd, outer))
        place = outer + index * length
        outside = jnp.where((place >= 0) & (place < grid), 0, 8)
        apart = jnp.abs(own - outer)
        same = same | apart
        code = code | jnp.where(apart > 1, 8, apart << a) | outside
        key = own + index * length if own_is_key else place
        bad = bad | jnp.where((key >= low) & (key <= high), 0, 8)
    code_ref[...] = code | jnp.where(same == 0, 0, bad)


NT = (((1,), (1,)), ((), ()))
NN = (((1,), (0,)), ((), ()))
TN = (((0,), (0,)), ((), ()))
STEP = 64


def dot(a, b, dims):
    return lax.dot_general(a, b, dims, preferred_element_type=jnp.float32)


def gather(groups, which, cols):
    parts = []
    for refs, pad in groups:
        parts += [r[which, :, cols] for r in refs]
        if pad:
            parts.append(jnp.zeros((pad, parts[0].shape[1]), parts[0].dtype))
    return jnp.concatenate(parts, axis=0)


def put_tiles(ref, value, cols):
    T, H, W, C, _ = ref.shape
    value = value.astype(ref.dtype)
    for w in range(W):
        for t in range(T):
            r = (w * T + t) * H * C
            ref[t, :, w, :, cols] = value[r : r + H * C].reshape(H, C, value.shape[1])


def products_kernel(cfg, closed_ref, code_ref, own_ref, *rest):
    depth, pad, first, own_is_key = cfg
    groups, (s_ref, g_ref) = [(rest[:-2], pad)], rest[-2:]
    factor = LOG2E / math.sqrt(depth)
    for h in range(s_ref.shape[0]):
        cols = slice(h * depth, (h + 1) * depth)
        own, outer = ([own_ref[i, :, cols] for i in (0, 1)], [gather(groups, i, cols) for i in (0, 1)])
        if own_is_key:
            code = code_ref[:, first : first + s_ref.shape[2]]
            scores, grads = (dot(a, b, NT) for a, b in zip(own, outer))
        else:
            code = code_ref[first : first + s_ref.shape[1], :]
            scores, grads = (dot(b, a, NT) for a, b in zip(own, outer))
        s_ref[h] = jnp.where((code & closed_ref[0:1, h : h + 1]) == 0, scores * factor, NEG)
        g_ref[h] = grads


def near_kernel(cfg, closed_ref, code_ref, own_ref, *rest):
    s_ref, g_ref, m_ref = rest[-3:]
    heads, wide, _ = s_ref.shape
    products_kernel(cfg, closed_ref, code_ref, own_ref, *rest[:-1])
    for h in range(heads):
        bands = range(0, wide, STEP)
        peak = functools.reduce(jnp.maximum, [s_ref[h, r : r + STEP, :] for r in bands])
        peak = jnp.max(peak, axis=0, keepdims=True)
        total = part = 0.0
        for r in bands:
            raised = jnp.exp2(s_ref[h, r : r + STEP, :] - peak)
            total = total + raised
            part = part + raised * g_ref[h, r : r + STEP, :]
        m_ref[h, 0:1, :] = peak
        m_ref[h, 1:2, :] = jnp.sum(total, axis=0, keepdims=True)
        m_ref[h, 2:3, :] = jnp.sum(part, axis=0, keepdims=True)


def statistics_kernel(cfg, block, faces, closed_ref, code_ref, near_m_ref, qd_ref, *rest):
    heads, depth, wide, pad, count = cfg
    far, rest = [(rest[:count], pad)], rest[count:]
    s_ref, g_ref, stat_rows, stat_ref = rest[:4]
    first_refs = rest[4:]
    stat_rows[...] = jnp.zeros(stat_rows.shape, jnp.float32)
    for h in range(heads):
        cols = slice(h * depth, (h + 1) * depth)
        scores = dot(gather(far, 0, cols), qd_ref[0, :, cols], NT) * (LOG2E / math.sqrt(depth))
        grads = dot(gather(far, 1, cols), qd_ref[1, :, cols], NT)
        allowed = (code_ref[wide:, :] & closed_ref[0:1, h : h + 1]) == 0
        scores = jnp.where(allowed, scores, NEG)
        s_ref[h] = scores
        g_ref[h] = grads
        near_peak = near_m_ref[h, 0:1, :]
        peak = jnp.maximum(near_peak, jnp.max(scores, axis=0, keepdims=True))
        raised = jnp.exp2(scores - peak)
        lower = jnp.exp2(near_peak - peak)
        total = near_m_ref[h, 1:2, :] * lower + jnp.sum(raised, axis=0, keepdims=True)
        part = near_m_ref[h, 2:3, :] * lower + jnp.sum(raised * grads, axis=0, keepdims=True)
        stat_rows[h : h + 1, :] = peak + jnp.log2(total)
        stat_rows[heads + h : heads + h + 1, :] = part / total
    stat_ref[0] = stat_rows[...].T
    T, H, W, C = block

    def put(k, t):
        for w in range(W):
            r = (w * T + t) * H * C
            first_refs[k][0, w * H * C : (w + 1) * H * C, :] = stat_ref[0, r : r + H * C, :]

    by_parity("ta", faces, T, put)


def query_kernel(cfg, near_s_ref, near_g_ref, far_s_ref, far_g_ref, stat_rows, *rest):
    heads, depth, pads, counts = cfg
    near, far = (rest[: counts[0]], pads[0]), (rest[counts[0] : sum(counts)], pads[1])
    dq_ref, d_ref = rest[sum(counts) :]
    wide, total_rows = near_s_ref.shape[1], d_ref.shape[1]
    for h in range(heads):
        cols = slice(h * depth, (h + 1) * depth)
        logsum = stat_rows[h : h + 1, :]
        drift = stat_rows[heads + h : heads + h + 1, :]
        for r in range(0, total_rows, STEP):
            i, s_ref, g_ref = (r, near_s_ref, near_g_ref) if r < wide else (r - wide, far_s_ref, far_g_ref)
            attention = jnp.exp2(s_ref[h, i : i + STEP, :] - logsum)
            d_ref[h % 2, r : r + STEP, :] = (
                attention * (g_ref[h, i : i + STEP, :] - drift)
            ).astype(jnp.bfloat16)
        product = dot(d_ref[h % 2], gather([near, far], 0, cols), TN) / math.sqrt(depth)
        put_tiles(dq_ref, product, cols)


def statistics_rows(st, pads, block, counts):
    T, H, W, C = block
    na, nh, nw = counts
    own, ta, near = st[0], st[1 : 1 + na], st[1 + na : 1 + na + nw]
    ha, far = st[1 + na + nw : 1 + na + nw + nh], st[1 + na + nw + nh :]
    a, each = T * C, (T + na) * C
    lines = [own[0]]
    lines += [r[0, w * each : w * each + a, :] for r in ha for w in range(W)]
    lines += [r[0] for r in ta]
    cut = T * H * C
    for n, f in zip(near, far):
        lines.append(n[0, :cut, :])
        lines += [f[0, k * each : k * each + a, :] for k in range(nh)]
        lines.append(n[0, cut:, :])
    if pads[0]:
        lines.append(jnp.zeros((pads[0], own.shape[2]), jnp.float32))
    lines += [r[0, w * each + a : (w + 1) * each, :] for r in ha for w in range(W)]
    lines += [f[0, k * each + a : (k + 1) * each, :] for f in far for k in range(nh)]
    if pads[1]:
        lines.append(jnp.zeros((pads[1], own.shape[2]), jnp.float32))
    return jnp.concatenate(lines, axis=0)


def key_kernel(cfg, *refs):
    heads, depth, pads, counts, parts, split, block, axes = cfg
    products, dq_ref, refs = refs[: 2 * parts], refs[2 * parts], refs[2 * parts + 1 :]
    near, far, refs = refs[: counts[0]], refs[counts[0] : sum(counts)], refs[sum(counts) :]
    qd = [(near, pads[0]), (far, pads[1])]
    st, refs = refs[: 1 + 2 * axes[2] + axes[0] + axes[1]], refs[-8:]
    dq_out, dk_out, dv_out, row_ref, dk_ref, dv_ref, dq_sem, sems = refs
    scale = 1.0 / math.sqrt(depth)
    row_ref[...] = statistics_rows(st, pads, block, axes).T
    copies = [pltpu.make_async_copy(dq_ref, dq_out, dq_sem)]
    copies[0].start()
    for h in range(heads):
        cols = slice(h * depth, (h + 1) * depth)
        scores = jnp.concatenate([r[h] for r in products[0::2]], axis=1)
        grads = jnp.concatenate([r[h] for r in products[1::2]], axis=1)
        attention = jnp.exp2(scores - row_ref[h : h + 1, :])
        drift = row_ref[heads + h : heads + h + 1, :]
        score_grads = (attention * (grads - drift)).astype(jnp.bfloat16)
        put_tiles(dk_ref, dot(score_grads, gather(qd, 0, cols), NN) * scale, cols)
        put_tiles(dv_ref, dot(attention.astype(jnp.bfloat16), gather(qd, 1, cols), NN), cols)
        if (h + 1) % (heads // split) == 0:
            i = (h + 1) // (heads // split) - 1
            done = slice((h + 1 - heads // split) * depth, (h + 1) * depth)
            for j, (ref, out) in enumerate(((dk_ref, dk_out), (dv_ref, dv_out))):
                copies.append(
                    pltpu.make_async_copy(
                        ref.at[:, :, :, :, done], out.at[:, :, :, :, done], sems.at[j, i]
                    )
                )
                copies[-1].start()
    for copy in copies:
        copy.wait()


def per_device(queries, key_states, value_states, output_cotangent, tile_valid, window_radius):
    T, H, W, C, width = queries.shape
    block = (T, H, W, C)
    heads = window_radius.shape[0]
    depth = width // heads
    sizes = tuple(lax.axis_size(a) for a in AXES)
    grids = tuple(n * b for n, b in zip(sizes, block))
    counts = tuple(len(matchings(a)) for a in AXES)
    rows = T * H * W * C

    kind = jax.ShapeDtypeStruct
    args = [
        pltpu.with_memory_space_constraint(x, pltpu.HBM)
        for x in (key_states, value_states, queries, output_cotangent)
    ]

    def prepared(pair, axes, name):
        plan = [(x, k) for x in axes for k in range(counts[AXES.index(x)])]
        made = local(
            functools.partial(prepare_kernel, block, plan),
            [pltpu.VMEM((2, W * C * (T if x == "ha" else H), width), jnp.bfloat16) for x, _ in plan]
            + [pltpu.VMEM((2, rows, width), jnp.bfloat16)],
            pair,
            space=pltpu.HBM,
            scratch_shapes=[
                pltpu.VMEM((2, T, H, W, C, width), jnp.bfloat16),
                pltpu.SemaphoreType.DMA((2, T)),
            ],
            name=name + "_prepare",
        )
        got, at = [], 0
        for x in axes:
            n = counts[AXES.index(x)]
            got.append(swap(x, made[at : at + n]))
            at += n
        return made[-1], got

    kv, (kv_ha, kv_ta) = prepared(args[:2], ("ha", "ta"), "kv")
    qd, (qd_ta, qd_ha) = prepared(args[2:], ("ta", "ha"), "qd")
    near, far = spread_early(kv, kv_ha, kv_ta, "ta", block, counts, "kv")
    qd_near, qd_far = spread_early(qd, qd_ha, qd_ta, "ha", block, counts, "qd")

    def table(axis):
        groups = piece_coords(block, counts, axis)
        pads = [-len(g) % 128 for g in groups]
        out = np.full((8, sum(len(g) + p for g, p in zip(groups, pads))), -(1 << 20), np.int32)
        at = 0
        for g, p in zip(groups, pads):
            out[:3, at : at + len(g)] = g.T
            at += len(g) + p
        return groups, pads, out

    groups, pads, outer_k = table("ta")
    _, pads_q, outer_q = table("ha")
    inner = np.zeros((8, rows), np.int32)
    inner[:3] = groups[0][:rows].T
    wide, all_wide = len(groups[0]) + pads[0], outer_k.shape[1]
    native = kind(queries.shape, jnp.bfloat16)
    lanes = -(-2 * heads // 128) * 128

    def codes(outer, own_is_key, name):
        tables = [inner, outer, tile_valid.transpose(0, 2, 1), window_radius.T]
        shape = (rows, all_wide) if own_is_key else (all_wide, rows)
        return local(
            functools.partial(codes_kernel, block, grids, own_is_key),
            [pltpu.VMEM(shape, jnp.int32), pltpu.VMEM((8, heads), jnp.int32)],
            [pltpu.with_memory_space_constraint(jnp.asarray(x), pltpu.HBM) for x in tables],
            space=pltpu.HBM,
            scratch_shapes=[pltpu.VMEM(x.shape, jnp.int32) for x in tables]
            + [pltpu.SemaphoreType.DMA((len(tables),))],
            name=name,
        )

    query_code, closed = codes(outer_k, False, "query_codes")
    key_code, key_closed = codes(outer_q, True, "key_codes")
    near_products = local(
        functools.partial(near_kernel, (depth, pads[0], 0, False)),
        [pltpu.VMEM((heads, wide, rows), jnp.float32)] * 2
        + [pltpu.VMEM((heads, 8, rows), jnp.float32)],
        [closed, query_code, qd] + near,
        name="query_products",
    )
    near_s, near_g, near_m = near_products
    made = local(
        functools.partial(
            statistics_kernel, (heads, depth, wide, pads[1], len(far)), block, counts[0]
        ),
        [pltpu.VMEM((heads, all_wide - wide, rows), jnp.float32)] * 2
        + [pltpu.VMEM((lanes, rows), jnp.float32), pltpu.VMEM((1, rows, lanes), jnp.float32)]
        + [pltpu.VMEM((1, W * H * C, lanes), jnp.float32)] * counts[0],
        [closed, query_code, near_m, qd] + far,
        name="query_statistics",
    )
    far_s, far_g, stat_rows, stats = made[:4]
    (query_gradient,) = local(
        functools.partial(query_kernel, (heads, depth, pads, (len(near), len(far)))),
        [pltpu.VMEM(queries.shape, jnp.bfloat16)],
        [near_s, near_g, far_s, far_g, stat_rows] + near + far,
        scratch_shapes=[pltpu.VMEM((2, all_wide, rows), jnp.bfloat16)],
        name="query_side",
    )
    st_ta = swap("ta", made[4:])
    stat_pieces = sum(spread(stats, st_ta, block, counts, "st"), [])
    products = []
    for i, pieces in enumerate((qd_near, qd_far)):
        products += local(
            functools.partial(products_kernel, (depth, pads_q[i], i * wide, True)),
            [pltpu.VMEM((heads, rows, all_wide - wide if i else wide), jnp.float32)] * 2,
            [key_closed, key_code, kv] + pieces,
            name=f"key_products_{i}",
        )
    split = math.gcd(heads, 6)
    lengths = (len(qd_near), len(qd_far))
    query_gradient, key_gradient, value_gradient = local(
        functools.partial(
            key_kernel, (heads, depth, pads_q, lengths, 2, split, block, counts)
        ),
        [native] * 3,
        products + [query_gradient] + qd_near + qd_far + stat_pieces,
        out_space=pltpu.HBM,
        scratch_shapes=[pltpu.VMEM((lanes, all_wide), jnp.float32)]
        + [pltpu.VMEM(queries.shape, jnp.bfloat16)] * 2
        + [pltpu.SemaphoreType.DMA, pltpu.SemaphoreType.DMA((2, split))],
        name="key_side",
    )
    return (query_gradient, key_gradient, value_gradient)


def solution(mesh):
    split = P("ta", "ha", "wa", None, None)

    return jax.shard_map(
        per_device,
        mesh=mesh,
        in_specs=(split, split, split, split, P(), P()),
        out_specs=(split, split, split),
        check_vma=False,
    )
```

```python
import functools
import math

import jax
import jax.numpy as jnp
import numpy as np
from jax import lax
from jax.experimental import pallas as pl
from jax.experimental.pallas import tpu as pltpu
from jax.sharding import PartitionSpec as P


NEG = -1e30
LOG2E = 1.4426950408889634
EVEN, ODD = 1000, 1001
AXES = ("ta", "ha", "wa")


def matchings(axis):
    n, m = lax.axis_size(axis), lax.axis_size("wa")
    if axis == "wa":
        sets = [[(i, i + 1) for i in range(k, n - 1, 2)] for k in range(2)]
        return [s + [(j, i) for i, j in s] for s in sets if s]
    sets = []
    for k in range(min(2, n - 1)):
        paired = [(i, i + 1) for i in range(k, n - 1, 2)]
        alone = sorted(set(range(n)) - {i for p in paired for i in p})
        pairs = [(i * m + w, j * m + w) for w in range(m) for i, j in paired]
        pairs += [(i * m + w, i * m + w + 1) for i in alone for w in range(0, m - 1, 2)]
        sets.append(pairs + [(j, i) for i, j in pairs])
    return sets


def swap(axis, sends):
    axes = axis if axis == "wa" else (axis, "wa")
    got = []
    for k, pairs in enumerate(matchings(axis)):
        got.append(lax.ppermute(sends[k], axes, pairs))
    return got


def sent_layer(axis, k, length):
    odd = lax.rem(lax.axis_index(axis), 2)
    return (1 - odd if k == 0 else odd) * (length - 1)


def by_parity(axis, count, length, put):
    odd = lax.rem(lax.axis_index(axis), 2)

    @pl.when(odd == 0)
    def _():
        for k in range(count):
            put(k, length - 1 if k == 0 else 0)

    @pl.when(odd == 1)
    def _():
        for k in range(count):
            put(k, 0 if k == 0 else length - 1)


def faces_kernel(block, count, *refs):
    T, H, W, C = block
    args, faces, (buf, sems) = refs[:2], refs[2 : 2 + count], refs[2 + count :]
    copies = {}
    for a in range(2):
        for k in range(count):
            source = args[a].at[:, sent_layer("ha", k, H)]
            copies[a, k] = pltpu.make_async_copy(source, buf.at[a, k], sems.at[a, k])
            copies[a, k].start()
    for (a, k), copy in copies.items():
        copy.wait()
        for w in range(W):
            faces[k][a, w * T * C : (w + 1) * T * C, :] = buf[a, k, :, w].reshape(
                T * C, buf.shape[-1]
            )


def prepare_kernel(block, plans, *refs):
    T, H, W, C = block
    args, outs, (buf, sems) = refs[: 2 * len(plans)], refs[2 * len(plans) : -2], refs[-2:]
    copies = [pltpu.make_async_copy(x, buf.at[a], sems.at[a]) for a, x in enumerate(args)]
    for copy in copies:
        copy.start()
    width = buf.shape[-1]
    for p, plan in enumerate(plans):
        whole, faces, outs = outs[0], outs[1 : 1 + len(plan)], outs[1 + len(plan) :]
        for i in range(2):
            a = 2 * p + i
            copies[a].wait()
            for w in range(W):
                for t in range(T):
                    r = (w * T + t) * H * C
                    whole[i, r : r + H * C, :] = buf[a, t, :, w].reshape(H * C, width)
                for face, (axis, k) in zip(faces, plan):
                    n = face.shape[1] // W
                    if axis == "ha":
                        layer = buf[a, :, sent_layer(axis, k, H), w]
                    else:
                        layer = buf[a, sent_layer(axis, k, T), :, w]
                    face[i, w * n : (w + 1) * n, :] = layer.reshape(n, width)


def corner_kernel(block, axis, near, count, *refs):
    T, H, W, C = block
    got, outs = refs[:near], refs[near:]
    other = T if axis == "ta" else H

    def put(k, layer):
        for a in range(got[0].shape[0]):
            for w in range(W):
                at = (w * other + layer) * C
                outs[k][a, w * near * C : (w + 1) * near * C, :] = jnp.concatenate(
                    [r[a, at : at + C, :] for r in got], axis=0
                )

    by_parity(axis, count, other, put)


def second_kernel(block, axis, near, count, own_ref, *refs):
    T, H, W, C = block
    got, outs = refs[:near], refs[near:]

    def put(k, layer):
        for a in range(own_ref.shape[0]):
            for w in range(W):
                if axis == "ta":
                    r = (w * T + layer) * H * C
                    parts = [own_ref[a, r : r + H * C, :]]
                    at = (w * T + layer) * C
                else:
                    parts = []
                    for t in range(T):
                        r = ((w * T + t) * H + layer) * C
                        parts.append(own_ref[a, r : r + C, :])
                    at = (w * H + layer) * C
                parts += [r[a, at : at + C, :] for r in got]
                n = outs[k].shape[1] // W
                outs[k][a, w * n : (w + 1) * n, :] = jnp.concatenate(parts, axis=0)

    by_parity(axis, count, T if axis == "ta" else H, put)


def column_kernel(block, count, *refs):
    _, _, W, _ = block
    pieces, outs = refs[: len(refs) - count], refs[len(refs) - count :]

    def put(k, w):
        for a in range(outs[k].shape[0]):
            at = 0
            for r in pieces:
                n = r.shape[1] // W
                outs[k][a, at : at + n, :] = r[a, w * n : (w + 1) * n, :]
                at += n

    by_parity("wa", count, W, put)


def local(kernel, out_shape, operands, space=pltpu.VMEM, out_space=pltpu.VMEM, **kw):
    place = pl.BlockSpec(memory_space=space)
    made = pl.pallas_call(
        kernel,
        out_shape=out_shape,
        in_specs=[place] * len(operands),
        out_specs=[pl.BlockSpec(memory_space=out_space)] * len(out_shape),
        compiler_params=pltpu.CompilerParams(vmem_limit_bytes=16 << 20),
        **kw,
    )(*operands)
    return list(made)


def column_swap(pieces, block, counts, name):
    k, _, width = pieces[0].shape
    n = sum(p.shape[1] for p in pieces) // block[2]
    sends = local(
        functools.partial(column_kernel, block, counts[2]),
        [pltpu.VMEM((k, n, width), pieces[0].dtype)] * counts[2],
        pieces,
        name=name,
    )
    return swap("wa", sends)


def spread(own, got, block, counts, name):
    T, _, W, C = block
    k, _, width = own.shape
    more = swap(
        "ha",
        local(
            functools.partial(second_kernel, block, "ha", counts[0], counts[1]),
            [pltpu.VMEM((k, W * (T + counts[0]) * C, width), own.dtype)] * counts[1],
            [own] + got,
            name=name + "_second",
        ),
    )
    near = column_swap([own] + got, block, counts, name + "_near")
    far = column_swap(more, block, counts, name + "_far")
    return [own], got, near, more, far


def spread_early(own, ha, ta, axis, block, counts, name):
    _, _, W, C = block
    k, _, width = own.shape
    got, near_count, count = (ha, counts[1], counts[0]) if axis == "ta" else (ta, counts[0], counts[1])
    corners = swap(
        axis,
        local(
            functools.partial(corner_kernel, block, axis, near_count, count),
            [pltpu.VMEM((k, W * near_count * C, width), own.dtype)] * count,
            got,
            name=name + "_corner",
        ),
    )
    near = [own] + ha + ta
    near += column_swap(near, block, counts, name + "_near")
    far = corners + column_swap(corners, block, counts, name + "_far")
    return near, far


def piece_coords(block, counts, axis):
    T, H, W, C = block
    marks = [(EVEN, ODD)[:n] for n in counts]
    ts, hs, ws = list(range(T)), list(range(H)), list(range(W))

    def piece(cells):
        return np.array([[cell + (w,) for cell in cells] for w in ws], np.int32)

    near = [piece([(t, h) for t in ts for h in hs])]
    near += [piece([(t, m) for t in ts]) for m in marks[1]]
    near += [piece([(m, h) for h in hs]) for m in marks[0]]
    if axis == "ta":
        far = [piece([(m, h) for h in marks[1]]) for m in marks[0]]
    else:
        far = [piece([(t, m) for t in marks[0]]) for m in marks[1]]
    groups = []
    for part in (near, far):
        column = np.concatenate([p[0] for p in part], axis=0)
        rows = [p.reshape(-1, 3) for p in part]
        for m in marks[2]:
            rows.append(column.copy())
            rows[-1][:, 2] = m
        groups.append(np.repeat(np.concatenate(rows, axis=0), C, axis=0))
    return groups


def codes_kernel(block, grids, own_is_key, *refs):
    sources, (code_ref, closed_ref), bufs, sems = refs[:4], refs[4:6], refs[6:10], refs[10]
    copies = [pltpu.make_async_copy(s, b, sems.at[i]) for i, (s, b) in enumerate(zip(sources, bufs))]
    for copy in copies:
        copy.start()
    for copy in copies:
        copy.wait()
    own_ref, outer_ref, valid_ref, radius_ref = bufs
    r = radius_ref[...]
    closed = 8 + (1 - r[0:1]) + 2 * (1 - r[1:2]) + 4 * (1 - r[2:3])
    closed_ref[...] = jnp.broadcast_to(closed, closed_ref.shape)
    own_all, outer_all = own_ref[...], outer_ref[...]
    if own_is_key:
        own_all = own_all.T
    else:
        outer_all = outer_all.T
    code = same = bad = 0
    for a, axis in enumerate(AXES):
        length, grid = block[a], grids[a]

        def line(i):
            i = i % grid
            if a == 0:
                return valid_ref[i, 1:2, 1:2]
            if a == 1:
                return valid_ref[1, 1:2, i : i + 1]
            return valid_ref[1, i : i + 1, 1:2]

        low = 1 - line(0)
        high = grid - 3 + line(-1) + line(-2)
        index = lax.axis_index(axis)
        odd = lax.rem(index, 2)
        at_even = jnp.where(odd == 1, -1, length)
        at_odd = jnp.where(odd == 1, length, -1)
        if own_is_key:
            own, outer = own_all[:, a : a + 1], outer_all[a : a + 1, :]
        else:
            own, outer = own_all[a : a + 1, :], outer_all[:, a : a + 1]
        outer = jnp.where(outer == EVEN, at_even, jnp.where(outer == ODD, at_odd, outer))
        place = outer + index * length
        outside = jnp.where((place >= 0) & (place < grid), 0, 8)
        apart = jnp.abs(own - outer)
        same = same | apart
        code = code | jnp.where(apart > 1, 8, apart << a) | outside
        key = own + index * length if own_is_key else place
        bad = bad | jnp.where((key >= low) & (key <= high), 0, 8)
    code_ref[...] = code | jnp.where(same == 0, 0, bad)


NT = (((1,), (1,)), ((), ()))
NN = (((1,), (0,)), ((), ()))
TN = (((0,), (0,)), ((), ()))
STEP = 64


def dot(a, b, dims):
    return lax.dot_general(a, b, dims, preferred_element_type=jnp.float32)


def gather(groups, which, cols):
    parts = []
    for refs, pad in groups:
        parts += [r[which, :, cols] for r in refs]
        if pad:
            parts.append(jnp.zeros((pad, parts[0].shape[1]), parts[0].dtype))
    return jnp.concatenate(parts, axis=0)


def put_tiles(ref, value, cols):
    T, H, W, C, _ = ref.shape
    value = value.astype(ref.dtype)
    for w in range(W):
        for t in range(T):
            r = (w * T + t) * H * C
            ref[t, :, w, :, cols] = value[r : r + H * C].reshape(H, C, value.shape[1])


def products_kernel(cfg, closed_ref, code_ref, own_ref, *rest):
    depth, pad, first, own_is_key = cfg
    groups, (s_ref, g_ref) = [(rest[:-2], pad)], rest[-2:]
    factor = LOG2E / math.sqrt(depth)
    for h in range(s_ref.shape[0]):
        cols = slice(h * depth, (h + 1) * depth)
        own, outer = ([own_ref[i, :, cols] for i in (0, 1)], [gather(groups, i, cols) for i in (0, 1)])
        if own_is_key:
            code = code_ref[:, first : first + s_ref.shape[2]]
            scores, grads = (dot(a, b, NT) for a, b in zip(own, outer))
        else:
            code = code_ref[first : first + s_ref.shape[1], :]
            scores, grads = (dot(b, a, NT) for a, b in zip(own, outer))
        s_ref[h] = jnp.where((code & closed_ref[0:1, h : h + 1]) == 0, scores * factor, NEG)
        g_ref[h] = grads


def near_kernel(cfg, closed_ref, code_ref, own_ref, *rest):
    s_ref, g_ref, m_ref = rest[-3:]
    heads, wide, _ = s_ref.shape
    products_kernel(cfg, closed_ref, code_ref, own_ref, *rest[:-1])
    for h in range(heads):
        bands = range(0, wide, STEP)
        peak = functools.reduce(jnp.maximum, [s_ref[h, r : r + STEP, :] for r in bands])
        peak = jnp.max(peak, axis=0, keepdims=True)
        total = part = 0.0
        for r in bands:
            raised = jnp.exp2(s_ref[h, r : r + STEP, :] - peak)
            total = total + raised
            part = part + raised * g_ref[h, r : r + STEP, :]
        m_ref[h, 0:1, :] = peak
        m_ref[h, 1:2, :] = jnp.sum(total, axis=0, keepdims=True)
        m_ref[h, 2:3, :] = jnp.sum(part, axis=0, keepdims=True)


def statistics_kernel(cfg, block, faces, closed_ref, code_ref, near_m_ref, qd_ref, *rest):
    heads, depth, wide, pad, count = cfg
    far, rest = [(rest[:count], pad)], rest[count:]
    s_ref, g_ref, stat_rows, stat_ref = rest[:4]
    first_refs = rest[4:]
    stat_rows[...] = jnp.zeros(stat_rows.shape, jnp.float32)
    for h in range(heads):
        cols = slice(h * depth, (h + 1) * depth)
        scores = dot(gather(far, 0, cols), qd_ref[0, :, cols], NT) * (LOG2E / math.sqrt(depth))
        grads = dot(gather(far, 1, cols), qd_ref[1, :, cols], NT)
        allowed = (code_ref[wide:, :] & closed_ref[0:1, h : h + 1]) == 0
        scores = jnp.where(allowed, scores, NEG)
        s_ref[h] = scores
        g_ref[h] = grads
        near_peak = near_m_ref[h, 0:1, :]
        peak = jnp.maximum(near_peak, jnp.max(scores, axis=0, keepdims=True))
        raised = jnp.exp2(scores - peak)
        lower = jnp.exp2(near_peak - peak)
        total = near_m_ref[h, 1:2, :] * lower + jnp.sum(raised, axis=0, keepdims=True)
        part = near_m_ref[h, 2:3, :] * lower + jnp.sum(raised * grads, axis=0, keepdims=True)
        stat_rows[h : h + 1, :] = peak + jnp.log2(total)
        stat_rows[heads + h : heads + h + 1, :] = part / total
    stat_ref[0] = stat_rows[...].T
    T, H, W, C = block

    def put(k, t):
        for w in range(W):
            r = (w * T + t) * H * C
            first_refs[k][0, w * H * C : (w + 1) * H * C, :] = stat_ref[0, r : r + H * C, :]

    by_parity("ta", faces, T, put)


def query_kernel(cfg, near_s_ref, near_g_ref, far_s_ref, far_g_ref, stat_rows, *rest):
    heads, depth, pads, counts = cfg
    near, far = (rest[: counts[0]], pads[0]), (rest[counts[0] : sum(counts)], pads[1])
    dq_ref, d_ref = rest[sum(counts) :]
    wide, total_rows = near_s_ref.shape[1], d_ref.shape[1]
    for h in range(heads):
        cols = slice(h * depth, (h + 1) * depth)
        logsum = stat_rows[h : h + 1, :]
        drift = stat_rows[heads + h : heads + h + 1, :]
        for r in range(0, total_rows, STEP):
            i, s_ref, g_ref = (r, near_s_ref, near_g_ref) if r < wide else (r - wide, far_s_ref, far_g_ref)
            attention = jnp.exp2(s_ref[h, i : i + STEP, :] - logsum)
            d_ref[h % 2, r : r + STEP, :] = (
                attention * (g_ref[h, i : i + STEP, :] - drift)
            ).astype(jnp.bfloat16)
        product = dot(d_ref[h % 2], gather([near, far], 0, cols), TN) / math.sqrt(depth)
        put_tiles(dq_ref, product, cols)


def statistics_rows(st, pads, block, counts):
    T, H, W, C = block
    na, nh, nw = counts
    own, ta, near = st[0], st[1 : 1 + na], st[1 + na : 1 + na + nw]
    ha, far = st[1 + na + nw : 1 + na + nw + nh], st[1 + na + nw + nh :]
    a, each = T * C, (T + na) * C
    lines = [own[0]]
    lines += [r[0, w * each : w * each + a, :] for r in ha for w in range(W)]
    lines += [r[0] for r in ta]
    cut = T * H * C
    for n, f in zip(near, far):
        lines.append(n[0, :cut, :])
        lines += [f[0, k * each : k * each + a, :] for k in range(nh)]
        lines.append(n[0, cut:, :])
    if pads[0]:
        lines.append(jnp.zeros((pads[0], own.shape[2]), jnp.float32))
    lines += [r[0, w * each + a : (w + 1) * each, :] for r in ha for w in range(W)]
    lines += [f[0, k * each + a : (k + 1) * each, :] for f in far for k in range(nh)]
    if pads[1]:
        lines.append(jnp.zeros((pads[1], own.shape[2]), jnp.float32))
    return jnp.concatenate(lines, axis=0)


def key_kernel(cfg, *refs):
    heads, depth, pads, counts, parts, split, block, axes = cfg
    products, dq_ref, refs = refs[: 2 * parts], refs[2 * parts], refs[2 * parts + 1 :]
    near, far, refs = refs[: counts[0]], refs[counts[0] : sum(counts)], refs[sum(counts) :]
    qd = [(near, pads[0]), (far, pads[1])]
    st, refs = refs[: 1 + 2 * axes[2] + axes[0] + axes[1]], refs[-8:]
    dq_out, dk_out, dv_out, row_ref, dk_ref, dv_ref, dq_sem, sems = refs
    scale = 1.0 / math.sqrt(depth)
    row_ref[...] = statistics_rows(st, pads, block, axes).T
    copies = [pltpu.make_async_copy(dq_ref, dq_out, dq_sem)]
    copies[0].start()
    for h in range(heads):
        cols = slice(h * depth, (h + 1) * depth)
        scores = jnp.concatenate([r[h] for r in products[0::2]], axis=1)
        grads = jnp.concatenate([r[h] for r in products[1::2]], axis=1)
        attention = jnp.exp2(scores - row_ref[h : h + 1, :])
        drift = row_ref[heads + h : heads + h + 1, :]
        score_grads = (attention * (grads - drift)).astype(jnp.bfloat16)
        put_tiles(dk_ref, dot(score_grads, gather(qd, 0, cols), NN) * scale, cols)
        put_tiles(dv_ref, dot(attention.astype(jnp.bfloat16), gather(qd, 1, cols), NN), cols)
        if (h + 1) % (heads // split) == 0:
            i = (h + 1) // (heads // split) - 1
            done = slice((h + 1 - heads // split) * depth, (h + 1) * depth)
            for j, (ref, out) in enumerate(((dk_ref, dk_out), (dv_ref, dv_out))):
                copies.append(
                    pltpu.make_async_copy(
                        ref.at[:, :, :, :, done], out.at[:, :, :, :, done], sems.at[j, i]
                    )
                )
                copies[-1].start()
    for copy in copies:
        copy.wait()


def per_device(queries, key_states, value_states, output_cotangent, tile_valid, window_radius):
    T, H, W, C, width = queries.shape
    block = (T, H, W, C)
    heads = window_radius.shape[0]
    depth = width // heads
    sizes = tuple(lax.axis_size(a) for a in AXES)
    grids = tuple(n * b for n, b in zip(sizes, block))
    counts = tuple(len(matchings(a)) for a in AXES)
    rows = T * H * W * C

    kind = jax.ShapeDtypeStruct
    args = [
        pltpu.with_memory_space_constraint(x, pltpu.HBM)
        for x in (key_states, value_states, queries, output_cotangent)
    ]

    na, nh = counts[:2]
    ha_face = pltpu.VMEM((2, W * T * C, width), jnp.bfloat16)
    ta_face = pltpu.VMEM((2, W * H * C, width), jnp.bfloat16)
    whole = pltpu.VMEM((2, rows, width), jnp.bfloat16)
    faces = local(
        functools.partial(faces_kernel, block, nh),
        [ha_face] * nh,
        args[:2],
        space=pltpu.HBM,
        scratch_shapes=[
            pltpu.VMEM((2, nh, T, W, C, width), jnp.bfloat16),
            pltpu.SemaphoreType.DMA((2, nh)),
        ],
        name="kv_faces",
    )
    kv_ha = swap("ha", faces)
    plans = ([("ta", k) for k in range(na)], [("ta", k) for k in range(na)])
    plans[1].extend(("ha", k) for k in range(nh))
    made = local(
        functools.partial(prepare_kernel, block, plans),
        [whole] + [ta_face] * na + [whole] + [ta_face] * na + [ha_face] * nh,
        args,
        space=pltpu.HBM,
        scratch_shapes=[
            pltpu.VMEM((4, T, H, W, C, width), jnp.bfloat16),
            pltpu.SemaphoreType.DMA((4,)),
        ],
        name="prepare",
    )
    kv, qd = made[0], made[1 + na]
    kv_ta = swap("ta", made[1 : 1 + na])
    qd_ta = swap("ta", made[2 + na : 2 + 2 * na])
    qd_ha = swap("ha", made[2 + 2 * na :])
    near, far = spread_early(kv, kv_ha, kv_ta, "ta", block, counts, "kv")
    qd_near, qd_far = spread_early(qd, qd_ha, qd_ta, "ha", block, counts, "qd")

    def table(axis):
        groups = piece_coords(block, counts, axis)
        pads = [-len(g) % 128 for g in groups]
        out = np.full((8, sum(len(g) + p for g, p in zip(groups, pads))), -(1 << 20), np.int32)
        at = 0
        for g, p in zip(groups, pads):
            out[:3, at : at + len(g)] = g.T
            at += len(g) + p
        return groups, pads, out

    groups, pads, outer_k = table("ta")
    _, pads_q, outer_q = table("ha")
    inner = np.zeros((8, rows), np.int32)
    inner[:3] = groups[0][:rows].T
    wide, all_wide = len(groups[0]) + pads[0], outer_k.shape[1]
    native = kind(queries.shape, jnp.bfloat16)
    lanes = -(-2 * heads // 128) * 128

    def codes(outer, own_is_key, name):
        tables = [inner, outer, tile_valid.transpose(0, 2, 1), window_radius.T]
        shape = (rows, all_wide) if own_is_key else (all_wide, rows)
        return local(
            functools.partial(codes_kernel, block, grids, own_is_key),
            [pltpu.VMEM(shape, jnp.int32), pltpu.VMEM((8, heads), jnp.int32)],
            [pltpu.with_memory_space_constraint(jnp.asarray(x), pltpu.HBM) for x in tables],
            space=pltpu.HBM,
            scratch_shapes=[pltpu.VMEM(x.shape, jnp.int32) for x in tables]
            + [pltpu.SemaphoreType.DMA((len(tables),))],
            name=name,
        )

    query_code, closed = codes(outer_k, False, "query_codes")
    key_code, key_closed = codes(outer_q, True, "key_codes")
    near_products = local(
        functools.partial(near_kernel, (depth, pads[0], 0, False)),
        [pltpu.VMEM((heads, wide, rows), jnp.float32)] * 2
        + [pltpu.VMEM((heads, 8, rows), jnp.float32)],
        [closed, query_code, qd] + near,
        name="query_products",
    )
    near_s, near_g, near_m = near_products
    made = local(
        functools.partial(
            statistics_kernel, (heads, depth, wide, pads[1], len(far)), block, counts[0]
        ),
        [pltpu.VMEM((heads, all_wide - wide, rows), jnp.float32)] * 2
        + [pltpu.VMEM((lanes, rows), jnp.float32), pltpu.VMEM((1, rows, lanes), jnp.float32)]
        + [pltpu.VMEM((1, W * H * C, lanes), jnp.float32)] * counts[0],
        [closed, query_code, near_m, qd] + far,
        name="query_statistics",
    )
    far_s, far_g, stat_rows, stats = made[:4]
    (query_gradient,) = local(
        functools.partial(query_kernel, (heads, depth, pads, (len(near), len(far)))),
        [pltpu.VMEM(queries.shape, jnp.bfloat16)],
        [near_s, near_g, far_s, far_g, stat_rows] + near + far,
        scratch_shapes=[pltpu.VMEM((2, all_wide, rows), jnp.bfloat16)],
        name="query_side",
    )
    st_ta = swap("ta", made[4:])
    stat_pieces = sum(spread(stats, st_ta, block, counts, "st"), [])
    products = []
    for i, pieces in enumerate((qd_near, qd_far)):
        products += local(
            functools.partial(products_kernel, (depth, pads_q[i], i * wide, True)),
            [pltpu.VMEM((heads, rows, all_wide - wide if i else wide), jnp.float32)] * 2,
            [key_closed, key_code, kv] + pieces,
            name=f"key_products_{i}",
        )
    split = heads
    lengths = (len(qd_near), len(qd_far))
    query_gradient, key_gradient, value_gradient = local(
        functools.partial(
            key_kernel, (heads, depth, pads_q, lengths, 2, split, block, counts)
        ),
        [native] * 3,
        products + [query_gradient] + qd_near + qd_far + stat_pieces,
        out_space=pltpu.HBM,
        scratch_shapes=[pltpu.VMEM((lanes, all_wide), jnp.float32)]
        + [pltpu.VMEM(queries.shape, jnp.bfloat16)] * 2
        + [pltpu.SemaphoreType.DMA, pltpu.SemaphoreType.DMA((2, split))],
        name="key_side",
    )
    return (query_gradient, key_gradient, value_gradient)


def solution(mesh):
    split = P("ta", "ha", "wa", None, None)

    return jax.shard_map(
        per_device,
        mesh=mesh,
        in_specs=(split, split, split, split, P(), P()),
        out_specs=(split, split, split),
        check_vma=False,
    )
```
